32 devices in a mesh: pair: 8 (over z, y), occ: 4 (over x, core).
Axes of the slice: x: 2, y: 2, z: 4, core: 2. Of those that a mesh axis runs over, the one named last changes fastest.
Arguments:
- half_ints: bfloat16 [2, 896, 4, 896], P(None, 'pair', 'occ'), may hold values from -6 to 6
- coeffs: bfloat16 [896, 768], P('occ'), may hold values from -0.1875 to 0.1875
- pair_map: int32 [8], replicated, may hold values from 0 to 7, each once
- tile_table: int32 [8], replicated, may hold values from 0 to 7, each once
Outputs:
- mo_ints: float32 [1536, 4, 768], P('pair', 'occ')
The draws below stay inside these ranges and needn't reach their ends.
Inputs may be any that keep to these rules, and one draw needn't show every extreme that they name: pair_map is a permutation of 0 to 7. tile_table is a permutation of 0 to 7.
All inputs are finite; a program needn't handle non-finite values.
Results may differ from the reference program's by a relative error of at most 0.0029.
Values may be sent and summed in bfloat16 or wider, within the bound.
A program may use at most 64 MiB of HBM per device.

```python
import jax
import jax.numpy as jnp

NBF = 896
NV = 768
I = 2
J = 4
N_PAIR = 8


def shard_levels(stream_key, dims, shards, smallest, largest):
    factor_of = 1.0
    for dim, parts in shards:
        steps = jax.random.uniform(jax.random.fold_in(jax.random.fold_in(stream_key, 6), dim), (parts,), jnp.float32, smallest / len(shards), largest / len(shards))
        factor_of = factor_of * jnp.repeat(jnp.exp(steps), dims[dim] // parts).reshape((-1,) + (1,) * (len(dims) - 1 - dim))
    return factor_of


def bell_draw(stream_key, extent, deviation, most, cuts=(), kind=jnp.bfloat16):
    entries = jax.random.normal(stream_key, extent, jnp.float32) * deviation
    if len(cuts) > 0:
        entries = shard_levels(stream_key, extent, cuts, -0.22, 0.18) * entries
    return jnp.clip(entries, min=-most, max=most).astype(kind)


def setup_inputs(seed: int = 0) -> dict:
    arg_keys = jax.random.split(jax.random.key(seed), 5)
    return {
        "half_ints": bell_draw(arg_keys[0], (I, NBF, J, NBF), 1.0, 6.0, ((1, 8), (2, 4))),
        "coeffs": bell_draw(arg_keys[1], (NBF, NV), NBF ** -0.5, 0.1875, ((0, 4),)),
        "pair_map": jax.random.permutation(arg_keys[2], N_PAIR).astype(jnp.int32),
        "tile_table": jax.random.permutation(arg_keys[3], N_PAIR).astype(jnp.int32),
    }


def reference(half_ints, coeffs, pair_map, tile_table):
    sblock = NBF // N_PAIR
    tile_rows = I * NV // N_PAIR
    split = half_ints.reshape(I, N_PAIR, sblock, J, NBF)
    natural = jnp.zeros_like(split).at[:, pair_map].set(split).reshape(I, NBF, J, NBF)
    half_mo = jnp.einsum("isjr,rb->isjb", natural.astype(jnp.float32), coeffs.astype(jnp.float32)).astype(jnp.bfloat16)
    full = jnp.einsum("sa,isjb->iajb", coeffs.astype(jnp.float32), half_mo.astype(jnp.float32))
    tiles = full.reshape(N_PAIR, tile_rows, J, NV)[tile_table]
    return tiles.reshape(I * NV, J, NV)
```

```python
import functools

import jax
import jax.numpy as jnp
from jax import lax
from jax.experimental import pallas as pl
from jax.experimental.pallas import tpu as pltpu
from jax.sharding import PartitionSpec as P


def shards_general(half_ints, coeffs, pair_map, tile_table):
    num_occ = half_ints.shape[0]
    sblock = half_ints.shape[1]
    local_j = half_ints.shape[2]
    num_basis = half_ints.shape[3]
    num_virt = coeffs.shape[1]
    num_pair = lax.axis_size("pair")
    tile_rows = num_occ * num_virt // num_pair
    all_coeffs = lax.all_gather(coeffs, "occ", axis=0, tiled=True)
    flat_ints = half_ints.reshape(num_occ * sblock * local_j, num_basis)
    half_mo = jnp.dot(flat_ints, all_coeffs, preferred_element_type=jnp.float32).astype(
        jnp.bfloat16
    )
    tile_id = jnp.sum(
        jnp.where(jnp.arange(num_pair) == lax.axis_index("pair"), tile_table, 0)
    )
    virt_start = tile_id * tile_rows % num_virt
    column_coeffs = lax.dynamic_slice_in_dim(all_coeffs, virt_start, tile_rows, 1)
    half_flat = half_mo.reshape(num_occ, sblock, local_j * num_virt)
    slot_occ = (tile_table * tile_rows // num_virt)[:, None, None]
    outgoing = jnp.broadcast_to(half_flat[:1], (num_pair,) + half_flat.shape[1:])
    for i in range(1, num_occ):
        outgoing = jnp.where(slot_occ == i, half_flat[i:i + 1], outgoing)
    incoming = lax.all_to_all(outgoing, "pair", split_axis=0, concat_axis=0, tiled=True)
    chosen = (pair_map[:, None] == jnp.arange(num_pair)[None, :]).astype(jnp.bfloat16)
    block_coeffs = jnp.einsum(
        "pg,gsa->psa", chosen, column_coeffs.reshape(num_pair, sblock, tile_rows),
        preferred_element_type=jnp.float32,
    ).astype(jnp.bfloat16)
    result = jnp.einsum("psa,psc->ac", block_coeffs, incoming, preferred_element_type=jnp.float32)
    return result.reshape(tile_rows, local_j, num_virt)


LANES = 128


def kernel(
    num_pair, num_i, local_tiles,
    pm_hbm, tt_hbm, h_hbm, c_hbm, o_ref,
    pm_ref, tt_ref, h_ref, c_all, ct,
    hs_wide, hr_wide, hs_slim, hr_slim, part, tiles_wide, tiles_slim, ts_wide, tr_wide, ts_slim, tr_slim,
    h_sem, c_sem, s_sem, x_send, x_recv, f_send, f_recv, p_send, p_recv,
    w1_send, w1_recv, n1_send, n1_recv, w2_send, w2_recv, n2_send, n2_recv,
):
    me = lax.axis_index("pair")
    occ = lax.axis_index("occ")
    num_z = num_pair // 2
    z, y = me // 2, lax.rem(me, 2)
    core = lax.rem(occ, 2)
    wide = lax.rem(y + core, 2) == 0
    slim = lax.rem(y + core, 2) == 1
    num_virt = c_hbm.shape[1]
    crows = c_hbm.shape[0]
    sblock = h_hbm.shape[0] // num_i
    tile_rows = num_virt // local_tiles
    half_rows = tile_rows // 2
    per_row = num_virt // LANES
    half = LANES // 2
    partner = occ + 1 - 2 * core
    cross = lax.rem(occ + 2, 4)
    diagonal = cross + 1 - 2 * core
    MESH = pl.DeviceIdType.MESH

    far_a, far_b, near, own = lax.rem(z + 2, 4), 3 - z, z + 1 - 2 * lax.rem(z, 2), z
    planes = (far_a, far_b, near, own)
    steps = (
        (far_a, True), (far_b, True), (num_z + 1 - z // 2, False),
        (near, True), (own, True), (num_z + z // 2, False),
    )

    def remote(source, target, send, recv, where):
        return pltpu.make_async_remote_copy(
            src_ref=source, dst_ref=target, send_sem=send, recv_sem=recv,
            device_id=where, device_id_type=MESH,
        )

    barrier = pltpu.get_barrier_semaphore()
    greeted = [{"occ": partner}, {"occ": cross}] + [
        {"pair": 2 * plane + lax.rem(y + dy, 2)} for plane in planes for dy in (0, 1)][:-2] + [
        {"pair": 2 * z + 1 - y}]
    for peer in greeted:
        pl.semaphore_signal(barrier, inc=1, device_id=peer, device_id_type=MESH)

    mine = pl.ds(crows * occ, crows)
    theirs = pl.ds(crows * cross, crows)
    fetch_c = [
        pltpu.make_async_copy(
            c_hbm.at[:, pl.ds(pl.multiple_of(m * LANES, LANES), LANES)], c_all.at[m, mine, :], c_sem.at[n])
        for n, (m, _) in enumerate(steps)]
    fetch_h = pltpu.make_async_copy(h_hbm, h_ref, h_sem)
    fetch_pm = pltpu.make_async_copy(pm_hbm, pm_ref, s_sem.at[0])
    fetch_tt = pltpu.make_async_copy(tt_hbm, tt_ref, s_sem.at[1])
    for fetch in fetch_c + [fetch_h, fetch_pm, fetch_tt]:
        fetch.start()

    to_cross, relay = [], []
    for n, (m, _) in enumerate(steps):
        spot = c_all.at[m, mine, :]
        to_cross.append(remote(spot, spot, x_send.at[n], x_recv.at[n], {"occ": cross}))
        spot = c_all.at[m, theirs, :]
        relay.append(remote(spot, spot, f_send.at[n], f_recv.at[n], {"occ": partner}))
    block = c_all.at[:, mine, :]
    to_partner = remote(block, block, p_send, p_recv, {"occ": partner})

    def send_wide(m):
        return remote(hs_wide.at[m], hr_wide.at[me], w1_send.at[m], w1_recv.at[me], {"pair": 2 * m + core})

    def send_slim(m):
        return remote(hs_slim.at[m], hr_slim.at[me], n1_send.at[m], n1_recv.at[me], {"pair": 2 * m + 1 - core})

    for fetch in fetch_c:
        fetch.wait()
    pl.semaphore_wait(barrier, len(greeted))
    to_cross[0].start()
    to_partner.start()
    for copy in to_cross[1:]:
        copy.start()

    def turn(m):
        for g in range(num_pair):
            ct[g, pl.ds(pl.multiple_of(m * LANES, LANES), LANES), :] = c_all[m, g * sblock:(g + 1) * sblock, :].T

    low = lax.broadcasted_iota(jnp.int32, (sblock, LANES), 1) < half

    fetch_h.wait()
    to_partner.wait_recv()
    for n, (m, is_wide) in enumerate(steps):
        to_cross[n].wait_recv()
        relay[n].start()
        if n > 0:
            turn(steps[n - 1][0])
        relay[n].wait_recv()
        prod = jnp.dot(h_ref[...], c_all[m], preferred_element_type=jnp.float32)
        first, second = prod[:sblock], prod[sblock:]
        if is_wide:
            hs_wide[m, 0] = first.astype(jnp.bfloat16)
            hs_wide[m, 1] = second.astype(jnp.bfloat16)
            if m is own:
                @pl.when(slim)
                def _():
                    send_wide(m).start()
            else:
                send_wide(m).start()
        else:
            base = 2 * (m - num_z)
            hs_slim[base] = jnp.where(low, first, pltpu.roll(second, half, 1)).astype(jnp.bfloat16)
            hs_slim[base + 1] = jnp.where(low, pltpu.roll(first, half, 1), second).astype(jnp.bfloat16)
            if n == 2:
                send_slim(far_a).start()
                send_slim(far_b).start()
            else:
                send_slim(near).start()

                @pl.when(wide)
                def _():
                    send_slim(own).start()
    turn(steps[-1][0])
    fetch_pm.wait()
    fetch_tt.wait()

    def sources(group):
        return [(2 * plane + lax.rem(y + dy, 2), plane is own and dy == 0) for plane in group for dy in (0, 1)]

    groups = (sources((far_a, far_b)), sources((near, own)))
    slots = sources(planes)
    cut = lax.broadcasted_iota(jnp.int32, (half_rows, LANES), 1) < half

    @pl.when(wide)
    def _():
        for g, group in enumerate(groups):
            for p, here in group:
                if not here:
                    remote(hs_wide.at[0], hr_wide.at[p], w1_send.at[0], w1_recv.at[p], {"pair": p}).wait_recv()
            for j in range(local_tiles):
                rows = slice(j * tile_rows, (j + 1) * tile_rows)
                total = part[rows, :] if g > 0 else None
                for p, here in group:
                    pieces = [hs_wide[z, i] if here else hr_wide[p, i] for i in range(num_i)]
                    term = jnp.dot(
                        ct[pm_ref[p], rows, :], jnp.concatenate(pieces, axis=1), preferred_element_type=jnp.float32)
                    total = term if total is None else total + term
                if g == 0:
                    part[rows, :] = total
                else:
                    for i in range(num_i):
                        tiles_wide[i * local_tiles + j] = total[:, i * LANES:(i + 1) * LANES].astype(jnp.bfloat16)
        for p, here in slots:
            if here:
                tr_wide[z] = tiles_wide[tt_ref[p]]
            else:
                ts_wide[p] = tiles_wide[tt_ref[p]]
                remote(ts_wide.at[p], tr_wide.at[z], w2_send.at[p], w2_recv.at[z], {"pair": p}).start()

    @pl.when(slim)
    def _():
        for g, group in enumerate(groups):
            for p, here in group:
                if not here:
                    remote(hs_slim.at[0], hr_slim.at[p], n1_send.at[0], n1_recv.at[p], {"pair": p}).wait_recv()
            for j in range(local_tiles):
                rows = slice(j * tile_rows, (j + 1) * tile_rows)
                total = part[rows, :LANES] if g > 0 else None
                for p, here in group:
                    piece = hs_slim[z] if here else hr_slim[p]
                    term = jnp.dot(ct[pm_ref[p], rows, :], piece, preferred_element_type=jnp.float32)
                    total = term if total is None else total + term
                if g == 0:
                    part[rows, :LANES] = total
                else:
                    top, bottom = total[:half_rows], total[half_rows:]
                    tiles_slim[j] = jnp.where(cut, top, pltpu.roll(bottom, half, 1)).astype(jnp.bfloat16)
                    tiles_slim[local_tiles + j] = jnp.where(
                        cut, pltpu.roll(top, half, 1), bottom).astype(jnp.bfloat16)
        for p, here in slots:
            if here:
                tr_slim[z] = tiles_slim[tt_ref[p]]
            else:
                ts_slim[p] = tiles_slim[tt_ref[p]]
                remote(ts_slim.at[p], tr_slim.at[z], n2_send.at[p], n2_recv.at[z], {"pair": p}).start()

    for m in range(num_z):
        @pl.when(jnp.logical_or(slim, z != m))
        def _():
            remote(ts_wide.at[0], tr_wide.at[m], w2_send.at[0], w2_recv.at[m], {"pair": 2 * m + core}).wait_recv()
        o_ref[pl.ds(m, tile_rows, stride=per_row), :] = tr_wide[m].astype(jnp.float32)
    for u in range(num_z // 2):
        for m in (2 * u, 2 * u + 1):
            @pl.when(jnp.logical_or(wide, z != m))
            def _():
                remote(ts_slim.at[0], tr_slim.at[m], n2_send.at[0], n2_recv.at[m], {"pair": 2 * m + 1 - core}).wait_recv()
        even, odd = tr_slim[2 * u].astype(jnp.float32), tr_slim[2 * u + 1].astype(jnp.float32)
        o_ref[pl.ds(num_z + u, half_rows, stride=per_row), :] = jnp.where(cut, even, pltpu.roll(odd, half, 1))
        o_ref[pl.ds(half_rows * per_row + num_z + u, half_rows, stride=per_row), :] = jnp.where(
            cut, pltpu.roll(even, half, 1), odd)

    for copy in to_cross + relay + [to_partner]:
        copy.wait_send()
    for plane in planes:
        if plane is own:
            pl.when(slim)(lambda: send_wide(own).wait_send())
            pl.when(wide)(lambda: send_slim(own).wait_send())
        else:
            send_wide(plane).wait_send()
            send_slim(plane).wait_send()

    @pl.when(wide)
    def _():
        for p, here in slots:
            if not here:
                remote(ts_wide.at[p], tr_wide.at[z], w2_send.at[p], w2_recv.at[z], {"pair": p}).wait_send()

    @pl.when(slim)
    def _():
        for p, here in slots:
            if not here:
                remote(ts_slim.at[p], tr_slim.at[z], n2_send.at[p], n2_recv.at[z], {"pair": p}).wait_send()


def shards_kernel(half_ints, coeffs, pair_map, tile_table):
    num_i, sblock, local_j, num_basis = half_ints.shape
    num_virt = coeffs.shape[1]
    num_pair = lax.axis_size("pair")
    num_z = num_pair // 2
    local_tiles = num_pair // num_i
    tile_rows = num_virt // local_tiles
    per_row = num_virt // LANES
    ints = half_ints.reshape(num_i * sblock, num_basis)
    bf16 = jnp.bfloat16
    dma = pltpu.SemaphoreType.DMA
    vmem = pl.BlockSpec(memory_space=pltpu.VMEM)
    hbm = pl.BlockSpec(memory_space=pltpu.HBM)
    ints, mine, pair_map, tile_table = (
        pltpu.with_memory_space_constraint(a, pltpu.HBM) for a in (ints, coeffs, pair_map, tile_table))
    out = pl.pallas_call(
        functools.partial(kernel, num_pair, num_i, local_tiles),
        out_shape=jax.ShapeDtypeStruct((tile_rows * per_row, LANES), jnp.float32),
        in_specs=[hbm, hbm, hbm, hbm],
        out_specs=vmem,
        scratch_shapes=[
            pltpu.SMEM(pair_map.shape, jnp.int32),
            pltpu.SMEM(tile_table.shape, jnp.int32),
            pltpu.VMEM(ints.shape, bf16),
            pltpu.VMEM((per_row, num_basis, LANES), bf16),
            pltpu.VMEM((num_pair, num_virt, sblock), bf16),
            pltpu.VMEM((num_z, num_i, sblock, LANES), bf16),
            pltpu.VMEM((num_pair, num_i, sblock, LANES), bf16),
            pltpu.VMEM((num_z, sblock, LANES), bf16),
            pltpu.VMEM((num_pair, sblock, LANES), bf16),
            pltpu.VMEM((num_virt, num_i * LANES), jnp.float32),
            pltpu.VMEM((num_pair, tile_rows, LANES), bf16),
            pltpu.VMEM((num_pair, tile_rows // 2, LANES), bf16),
            pltpu.VMEM((num_pair, tile_rows, LANES), bf16),
            pltpu.VMEM((num_z, tile_rows, LANES), bf16),
            pltpu.VMEM((num_pair, tile_rows // 2, LANES), bf16),
            pltpu.VMEM((num_z, tile_rows // 2, LANES), bf16),
            dma, dma((per_row,)), dma((2,)),
            dma((per_row,)), dma((per_row,)), dma((per_row,)), dma((per_row,)),
            dma, dma,
            dma((num_z,)), dma((num_pair,)), dma((num_z,)), dma((num_pair,)),
            dma((num_pair,)), dma((num_z,)), dma((num_pair,)), dma((num_z,)),
        ],
        compiler_params=pltpu.CompilerParams(
            collective_id=0, has_side_effects=True, vmem_limit_bytes=40 * 1024 * 1024),
    )(pair_map, tile_table, ints, mine)
    return out.reshape(tile_rows, local_j, num_virt)


def shards(half_ints, coeffs, pair_map, tile_table):
    num_i, sblock, local_j, num_basis = half_ints.shape
    num_virt = coeffs.shape[1]
    num_pair = lax.axis_size("pair")
    fits = (
        num_i == 2 and local_j == 1 and lax.axis_size("occ") == 4 and num_pair == 8
        and sblock % 16 == 0 and sblock <= LANES and sblock * num_pair == num_basis
        and coeffs.shape[0] * 4 == num_basis and coeffs.shape[0] % 16 == 0
        and num_virt * 4 == 3 * LANES * num_pair and num_virt % (32 * (num_pair // num_i)) == 0
    )
    body = shards_kernel if fits else shards_general
    return body(half_ints, coeffs, pair_map, tile_table)


def solution(mesh):
    placed = (P(None, "pair", "occ", None), P("occ", None), P(), P())
    return jax.shard_map(
        shards, mesh=mesh, in_specs=placed, out_specs=P("pair", "occ", None), check_vma=False
    )
```

```python
import functools

import jax
import jax.numpy as jnp
from jax import lax
from jax.experimental import pallas as pl
from jax.experimental.pallas import tpu as pltpu
from jax.sharding import PartitionSpec as P


def shards_general(half_ints, coeffs, pair_map, tile_table):
    num_occ = half_ints.shape[0]
    sblock = half_ints.shape[1]
    local_j = half_ints.shape[2]
    num_basis = half_ints.shape[3]
    num_virt = coeffs.shape[1]
    num_pair = lax.axis_size("pair")
    tile_rows = num_occ * num_virt // num_pair
    all_coeffs = lax.all_gather(coeffs, "occ", axis=0, tiled=True)
    flat_ints = half_ints.reshape(num_occ * sblock * local_j, num_basis)
    half_mo = jnp.dot(flat_ints, all_coeffs, preferred_element_type=jnp.float32).astype(
        jnp.bfloat16
    )
    tile_id = jnp.sum(
        jnp.where(jnp.arange(num_pair) == lax.axis_index("pair"), tile_table, 0)
    )
    virt_start = tile_id * tile_rows % num_virt
    column_coeffs = lax.dynamic_slice_in_dim(all_coeffs, virt_start, tile_rows, 1)
    half_flat = half_mo.reshape(num_occ, sblock, local_j * num_virt)
    slot_occ = (tile_table * tile_rows // num_virt)[:, None, None]
    outgoing = jnp.broadcast_to(half_flat[:1], (num_pair,) + half_flat.shape[1:])
    for i in range(1, num_occ):
        outgoing = jnp.where(slot_occ == i, half_flat[i:i + 1], outgoing)
    incoming = lax.all_to_all(outgoing, "pair", split_axis=0, concat_axis=0, tiled=True)
    chosen = (pair_map[:, None] == jnp.arange(num_pair)[None, :]).astype(jnp.bfloat16)
    block_coeffs = jnp.einsum(
        "pg,gsa->psa", chosen, column_coeffs.reshape(num_pair, sblock, tile_rows),
        preferred_element_type=jnp.float32,
    ).astype(jnp.bfloat16)
    result = jnp.einsum("psa,psc->ac", block_coeffs, incoming, preferred_element_type=jnp.float32)
    return result.reshape(tile_rows, local_j, num_virt)


LANES = 128


def kernel(
    num_pair, num_i, local_tiles,
    pm_hbm, tt_hbm, h_hbm, c_hbm, o_ref,
    pm_ref, tt_ref, c_all, ct, hs, hr, xs, tiles, ts, tr, out_sum,
    h_sem, c_sem, s_sem, x_send, x_recv, f_send, f_recv, p_send, p_recv,
    h_send, h_recv, t_send, t_recv,
):
    me = lax.axis_index("pair")
    occ = lax.axis_index("occ")
    z, y = me // 2, lax.rem(me, 2)
    core = lax.rem(occ, 2)
    num_basis, num_virt = c_all.shape
    crows = c_hbm.shape[0]
    sblock = h_hbm.shape[1]
    tile_rows = num_virt // local_tiles
    per_row = num_virt // LANES
    num_cols = num_basis // LANES
    middle = num_cols // 2
    partner = occ + 1 - 2 * core
    cross = lax.rem(occ + 2, 4)
    MESH = pl.DeviceIdType.MESH

    def column(plane, line):
        place = 2 * lax.rem(plane, 2) + lax.rem(line + core, 2)
        return middle + (2 * (plane // 2) - 1) * place

    mine = column(z, y)
    shared = mine == middle
    far_planes = (lax.rem(z + 2, 4), 3 - z)
    near_plane = z + 1 - 2 * lax.rem(z, 2)
    far = [(plane, line) for plane in far_planes for line in (y, 1 - y)]
    near = [(near_plane, y), (near_plane, 1 - y), (z, 1 - y)]
    peers = [(2 * plane + line, column(plane, line), n < len(far)) for n, (plane, line) in enumerate(far + near)]

    def remote(source, target, send, recv, where):
        return pltpu.make_async_remote_copy(
            src_ref=source, dst_ref=target, send_sem=send, recv_sem=recv,
            device_id=where, device_id_type=MESH,
        )

    barrier = pltpu.get_barrier_semaphore()
    greeted = [{"occ": partner}, {"occ": cross}] + [{"pair": p} for p, _, _ in peers]
    for peer in greeted:
        pl.semaphore_signal(barrier, inc=1, device_id=peer, device_id_type=MESH)

    mine_rows = pl.ds(pl.multiple_of(crows * occ, crows), crows)
    cross_rows = pl.ds(pl.multiple_of(crows * cross, crows), crows)

    def cols(m):
        return pl.ds(m * LANES, LANES)

    def h_column(m):
        return h_hbm.at[:, :, pl.ds(pl.multiple_of(m * LANES, LANES), LANES)]

    fetch_c = [
        pltpu.make_async_copy(c_hbm.at[:, cols(m)], c_all.at[mine_rows, cols(m)], c_sem.at[m])
        for m in range(per_row)]
    fetch_h = [
        pltpu.make_async_copy(h_column(m), hs.at[n], h_sem.at[n]) for n, (_, m, _) in enumerate(peers)]
    fetch_own = pltpu.make_async_copy(h_column(mine), hr.at[me], h_sem.at[len(peers)])
    fetch_pm = pltpu.make_async_copy(pm_hbm, pm_ref, s_sem.at[0])
    fetch_tt = pltpu.make_async_copy(tt_hbm, tt_ref, s_sem.at[1])
    for fetch in fetch_h + fetch_c + [fetch_own, fetch_pm, fetch_tt]:
        fetch.start()

    to_cross, relay = [], []
    for m in range(per_row):
        spot = c_all.at[mine_rows, cols(m)]
        to_cross.append(remote(spot, spot, x_send.at[m], x_recv.at[m], {"occ": cross}))
        spot = c_all.at[cross_rows, cols(m)]
        relay.append(remote(spot, spot, f_send.at[m], f_recv.at[m], {"occ": partner}))
    block = c_all.at[mine_rows, :]
    to_partner = remote(block, block, p_send, p_recv, {"occ": partner})
    h_copies = [
        remote(hs.at[n], hr.at[me], h_send.at[n], h_recv.at[me], {"pair": p}) for n, (p, _, _) in enumerate(peers)]
    h_arrivals = [
        remote(hs.at[n], hr.at[p], h_send.at[n], h_recv.at[p], {"pair": p}) for n, (p, _, _) in enumerate(peers)]
    t_copies = [
        remote(ts.at[n], tr.at[mine], t_send.at[n], t_recv.at[mine], {"pair": p}) for n, (p, _, _) in enumerate(peers)]
    t_arrivals = [
        remote(ts.at[n], tr.at[m], t_send.at[n], t_recv.at[m], {"pair": p}) for n, (p, m, _) in enumerate(peers)]

    for fetch in fetch_c + fetch_h:
        fetch.wait()
    pl.semaphore_wait(barrier, len(greeted))
    to_cross[0].start()
    for copy in h_copies[:len(far)]:
        copy.start()
    for copy in to_cross[1:]:
        copy.start()
    to_partner.start()
    for copy in h_copies[len(far):]:
        copy.start()

    def turn(m):
        ct[m * LANES:(m + 1) * LANES, :] = c_all[:, m * LANES:(m + 1) * LANES].T

    def transform(first, last):
        rows = slice(first * LANES, last * LANES)
        total = jnp.dot(ct[rows, :], xs[...], preferred_element_type=jnp.float32).astype(jnp.bfloat16)
        row = first * LANES
        while row < last * LANES:
            j, start = row // tile_rows, row % tile_rows
            end = min(tile_rows, start + last * LANES - row)
            piece = total[row - first * LANES:row - first * LANES + end - start]
            for i in range(num_i):
                tiles[i * local_tiles + j, start:end, :] = piece[:, i * LANES:(i + 1) * LANES]
            row += end - start

    for fetch in (fetch_own, fetch_pm, fetch_tt):
        fetch.wait()
    slot = []
    for g in range(num_pair):
        found = 0
        for p in range(1, num_pair):
            found = jnp.where(pm_ref[p] == g, p, found)
        slot.append(found)
    to_partner.wait_recv()
    early = per_row - 2
    for m in range(per_row):
        to_cross[m].wait_recv()
        relay[m].start()
        if m == early:
            for copy in h_arrivals:
                copy.wait_recv()
            for g in range(num_pair):
                for i in range(num_i):
                    xs[g * sblock:(g + 1) * sblock, i * LANES:(i + 1) * LANES] = hr[slot[g], i]
            transform(0, early)
        relay[m].wait_recv()
        turn(m)
        if m >= early:
            transform(m, m + 1)

    def tile(p):
        return tiles[tt_ref[p]]

    @pl.when(jnp.logical_not(shared))
    def _():
        for n in range(len(far)):
            ts[n] = tile(peers[n][0])
            t_copies[n].start()
    for n in range(len(far), len(peers)):
        ts[n] = tile(peers[n][0])
        t_copies[n].start()
    tr[mine] = tile(me)

    own_base = (z // 2) * middle
    far_base = (1 - z // 2) * (middle + 1)
    wide = 2 * LANES
    for g, (base, count, arrivals) in enumerate((
            (own_base, middle + 1, range(len(far), len(peers))), (far_base, middle, range(len(far))))):
        for n in arrivals:
            if g == 1:
                pl.when(peers[n][1] != middle)(t_arrivals[n].wait_recv)
            else:
                t_arrivals[n].wait_recv()
        left = jnp.concatenate([tr[base + u] for u in range(count)], axis=1)
        rows = pl.ds(pl.multiple_of(base * LANES, LANES), count * LANES)
        for n in range(num_virt // wide):
            span = slice(n * wide, (n + 1) * wide)
            total = jnp.dot(left, c_all[rows, span], preferred_element_type=jnp.float32)
            if g == 0:
                out_sum[:, span] = total
            else:
                total = total + out_sum[:, span]
                for m in range(2):
                    o_ref[pl.ds(2 * n + m, tile_rows, stride=per_row), :] = total[:, m * LANES:(m + 1) * LANES]

    for copy in to_cross + relay + [to_partner] + h_copies + t_copies[len(far):]:
        copy.wait_send()

    @pl.when(jnp.logical_not(shared))
    def _():
        for copy in t_copies[:len(far)]:
            copy.wait_send()


def shards_kernel(half_ints, coeffs, pair_map, tile_table):
    num_i, sblock, local_j, num_basis = half_ints.shape
    num_virt = coeffs.shape[1]
    num_pair = lax.axis_size("pair")
    local_tiles = num_pair // num_i
    tile_rows = num_virt // local_tiles
    per_row = num_virt // LANES
    num_cols = num_basis // LANES
    ints = half_ints.reshape(num_i, sblock, num_basis)
    bf16 = jnp.bfloat16
    dma = pltpu.SemaphoreType.DMA
    vmem = pl.BlockSpec(memory_space=pltpu.VMEM)
    hbm = pl.BlockSpec(memory_space=pltpu.HBM)
    ints, mine, pair_map, tile_table = (
        pltpu.with_memory_space_constraint(a, pltpu.HBM) for a in (ints, coeffs, pair_map, tile_table))
    out = pl.pallas_call(
        functools.partial(kernel, num_pair, num_i, local_tiles),
        out_shape=jax.ShapeDtypeStruct((tile_rows * per_row, LANES), jnp.float32),
        in_specs=[hbm, hbm, hbm, hbm],
        out_specs=vmem,
        scratch_shapes=[
            pltpu.SMEM(pair_map.shape, jnp.int32),
            pltpu.SMEM(tile_table.shape, jnp.int32),
            pltpu.VMEM((num_basis, num_virt), bf16),
            pltpu.VMEM((num_virt, num_basis), bf16),
            pltpu.VMEM((num_pair - 1, num_i, sblock, LANES), bf16),
            pltpu.VMEM((num_pair, num_i, sblock, LANES), bf16),
            pltpu.VMEM((num_basis, num_i * LANES), bf16),
            pltpu.VMEM((num_pair, tile_rows, LANES), bf16),
            pltpu.VMEM((num_pair - 1, tile_rows, LANES), bf16),
            pltpu.VMEM((num_cols, tile_rows, LANES), bf16),
            pltpu.VMEM((tile_rows, num_virt), jnp.float32),
            dma((num_pair,)), dma((per_row,)), dma((2,)),
            dma((per_row,)), dma((per_row,)), dma((per_row,)), dma((per_row,)),
            dma, dma,
            dma((num_pair - 1,)), dma((num_pair,)), dma((num_pair - 1,)), dma((num_cols,)),
        ],
        compiler_params=pltpu.CompilerParams(
            collective_id=0, has_side_effects=True, vmem_limit_bytes=40 * 1024 * 1024),
    )(pair_map, tile_table, ints, mine)
    return out.reshape(tile_rows, local_j, num_virt)


def shards(half_ints, coeffs, pair_map, tile_table):
    num_i, sblock, local_j, num_basis = half_ints.shape
    num_virt = coeffs.shape[1]
    num_pair = lax.axis_size("pair")
    fits = (
        num_i == 2 and local_j == 1 and lax.axis_size("occ") == 4 and num_pair == 8
        and sblock % 16 == 0 and sblock * num_pair == num_basis and num_basis == 7 * LANES
        and coeffs.shape[0] * 4 == num_basis and coeffs.shape[0] % 16 == 0
        and num_virt % (2 * LANES) == 0 and num_virt >= 4 * LANES and num_virt % (16 * (num_pair // num_i)) == 0
    )
    body = shards_kernel if fits else shards_general
    return body(half_ints, coeffs, pair_map, tile_table)


def solution(mesh):
    placed = (P(None, "pair", "occ", None), P("occ", None), P(), P())
    return jax.shard_map(
        shards, mesh=mesh, in_specs=placed, out_specs=P("pair", "occ", None), check_vma=False
    )
```

```python
import functools

import jax
import jax.numpy as jnp
from jax import lax
from jax.experimental import pallas as pl
from jax.experimental.pallas import tpu as pltpu
from jax.sharding import PartitionSpec as P


def shards_general(half_ints, coeffs, pair_map, tile_table):
    num_occ = half_ints.shape[0]
    sblock = half_ints.shape[1]
    local_j = half_ints.shape[2]
    num_basis = half_ints.shape[3]
    num_virt = coeffs.shape[1]
    num_pair = lax.axis_size("pair")
    tile_rows = num_occ * num_virt // num_pair
    all_coeffs = lax.all_gather(coeffs, "occ", axis=0, tiled=True)
    flat_ints = half_ints.reshape(num_occ * sblock * local_j, num_basis)
    half_mo = jnp.dot(flat_ints, all_coeffs, preferred_element_type=jnp.float32).astype(
        jnp.bfloat16
    )
    tile_id = jnp.sum(
        jnp.where(jnp.arange(num_pair) == lax.axis_index("pair"), tile_table, 0)
    )
    virt_start = tile_id * tile_rows % num_virt
    column_coeffs = lax.dynamic_slice_in_dim(all_coeffs, virt_start, tile_rows, 1)
    half_flat = half_mo.reshape(num_occ, sblock, local_j * num_virt)
    slot_occ = (tile_table * tile_rows // num_virt)[:, None, None]
    outgoing = jnp.broadcast_to(half_flat[:1], (num_pair,) + half_flat.shape[1:])
    for i in range(1, num_occ):
        outgoing = jnp.where(slot_occ == i, half_flat[i:i + 1], outgoing)
    incoming = lax.all_to_all(outgoing, "pair", split_axis=0, concat_axis=0, tiled=True)
    chosen = (pair_map[:, None] == jnp.arange(num_pair)[None, :]).astype(jnp.bfloat16)
    block_coeffs = jnp.einsum(
        "pg,gsa->psa", chosen, column_coeffs.reshape(num_pair, sblock, tile_rows),
        preferred_element_type=jnp.float32,
    ).astype(jnp.bfloat16)
    result = jnp.einsum("psa,psc->ac", block_coeffs, incoming, preferred_element_type=jnp.float32)
    return result.reshape(tile_rows, local_j, num_virt)


LANES = 128


def kernel(
    num_pair, num_i, local_tiles,
    pm_hbm, tt_hbm, h_hbm, c_hbm, o_ref,
    pm_ref, tt_ref, c_all, ct, hs, hr, ts, tr, out_sum,
    h_sem, c_sem, s_sem, x_send, x_recv, f_send, f_recv, p_send, p_recv,
    h_send, h_recv, t_send, t_recv,
):
    me = lax.axis_index("pair")
    occ = lax.axis_index("occ")
    z, y = me // 2, lax.rem(me, 2)
    core = lax.rem(occ, 2)
    num_basis, num_virt = c_all.shape
    crows = c_hbm.shape[0]
    sblock = h_hbm.shape[1]
    tile_rows = num_virt // local_tiles
    per_row = num_virt // LANES
    num_cols = num_basis // LANES
    middle = num_cols // 2
    partner = occ + 1 - 2 * core
    cross = lax.rem(occ + 2, 4)
    MESH = pl.DeviceIdType.MESH

    def column(plane, line):
        place = 2 * lax.rem(plane, 2) + lax.rem(line + core, 2)
        return middle + (2 * (plane // 2) - 1) * place

    mine = column(z, y)
    shared = mine == middle
    far_planes = (lax.rem(z + 2, 4), 3 - z)
    near_plane = z + 1 - 2 * lax.rem(z, 2)
    far = [(plane, line) for line in (1 - y, y) for plane in far_planes]
    near = [(near_plane, 1 - y), (z, 1 - y), (near_plane, y)]
    peers = [(2 * plane + line, column(plane, line)) for plane, line in far + near]

    def remote(source, target, send, recv, where):
        return pltpu.make_async_remote_copy(
            src_ref=source, dst_ref=target, send_sem=send, recv_sem=recv,
            device_id=where, device_id_type=MESH,
        )

    barrier = pltpu.get_barrier_semaphore()
    greeted = [{"occ": partner}, {"occ": cross}] + [{"pair": p} for p, _ in peers]
    for peer in greeted:
        pl.semaphore_signal(barrier, inc=1, device_id=peer, device_id_type=MESH)

    mine_rows = pl.ds(pl.multiple_of(crows * occ, crows), crows)
    cross_rows = pl.ds(pl.multiple_of(crows * cross, crows), crows)

    def cols(m):
        return pl.ds(m * LANES, LANES)

    def h_column(m):
        return h_hbm.at[:, :, pl.ds(pl.multiple_of(m * LANES, LANES), LANES)]

    fetch_c = [
        pltpu.make_async_copy(c_hbm.at[:, cols(m)], c_all.at[mine_rows, cols(m)], c_sem.at[m])
        for m in range(per_row)]
    fetch_h = [
        pltpu.make_async_copy(h_column(m), hs.at[n], h_sem.at[n]) for n, (_, m) in enumerate(peers)]
    fetch_own = pltpu.make_async_copy(h_column(mine), hr.at[me], h_sem.at[len(peers)])
    fetch_pm = pltpu.make_async_copy(pm_hbm, pm_ref, s_sem.at[0])
    fetch_tt = pltpu.make_async_copy(tt_hbm, tt_ref, s_sem.at[1])
    for fetch in fetch_h + fetch_c + [fetch_own, fetch_pm, fetch_tt]:
        fetch.start()

    to_cross, relay = [], []
    for m in range(per_row):
        spot = c_all.at[mine_rows, cols(m)]
        to_cross.append(remote(spot, spot, x_send.at[m], x_recv.at[m], {"occ": cross}))
        spot = c_all.at[cross_rows, cols(m)]
        relay.append(remote(spot, spot, f_send.at[m], f_recv.at[m], {"occ": partner}))
    block = c_all.at[mine_rows, :]
    to_partner = remote(block, block, p_send, p_recv, {"occ": partner})
    h_copies = [
        remote(hs.at[n], hr.at[me], h_send.at[n], h_recv.at[me], {"pair": p}) for n, (p, _) in enumerate(peers)]
    h_arrivals = [
        remote(hs.at[n], hr.at[p], h_send.at[n], h_recv.at[p], {"pair": p}) for n, (p, _) in enumerate(peers)]
    t_copies = [
        remote(ts.at[p], tr.at[mine], t_send.at[p], t_recv.at[mine], {"pair": jnp.int32(p)}) for p in range(num_pair)]
    t_arrivals = [
        remote(ts.at[p], tr.at[m], t_send.at[p], t_recv.at[m], {"pair": p}) for p, m in peers]

    for fetch in fetch_c + fetch_h:
        fetch.wait()
    pl.semaphore_wait(barrier, len(greeted))
    to_cross[0].start()
    for copy in h_copies[:2]:
        copy.start()
    for copy in to_cross[1:]:
        copy.start()
    to_partner.start()
    for copy in h_copies[2:]:
        copy.start()

    def turn(m):
        row = m * LANES
        while row < (m + 1) * LANES:
            j, start = row // tile_rows, row % tile_rows
            count = min(tile_rows - start, (m + 1) * LANES - row)
            ct[j, start:start + count, :] = c_all[:, m * LANES:(m + 1) * LANES].T[row - m * LANES:row - m * LANES + count]
            row += count

    for fetch in (fetch_own, fetch_pm, fetch_tt):
        fetch.wait()
    slot = []
    for g in range(num_pair):
        found = 0
        for p in range(1, num_pair):
            found = jnp.where(pm_ref[p] == g, p, found)
        slot.append(found)
    to_partner.wait_recv()
    for m in range(per_row):
        to_cross[m].wait_recv()
        relay[m].start()
        if m > 0:
            turn(m - 1)
        relay[m].wait_recv()
    turn(per_row - 1)
    for copy in h_arrivals:
        copy.wait_recv()

    def tile(p):
        t = tt_ref[p]
        i = jnp.where(t >= local_tiles, 1, 0)
        block = jnp.concatenate([hr[slot[g], i] for g in range(num_pair)], axis=0)
        return jnp.dot(ct[t - local_tiles * i], block, preferred_element_type=jnp.float32).astype(jnp.bfloat16)

    def sends(p):
        away = z // 2 != p // (num_pair // 2)
        return jnp.logical_and(me != p, jnp.logical_not(jnp.logical_and(shared, away)))

    for p in range(num_pair):
        @pl.when(sends(p))
        def _():
            ts[p] = tile(p)
            t_copies[p].start()
    tr[mine] = tile(me)

    own_base = (z // 2) * middle
    far_base = (1 - z // 2) * (middle + 1)
    wide = 2 * LANES
    for g, (base, count, arrivals) in enumerate((
            (own_base, middle + 1, range(len(far), len(peers))), (far_base, middle, range(len(far))))):
        for n in arrivals:
            if g == 1:
                pl.when(peers[n][1] != middle)(t_arrivals[n].wait_recv)
            else:
                t_arrivals[n].wait_recv()
        left = jnp.concatenate([tr[base + u] for u in range(count)], axis=1)
        rows = pl.ds(pl.multiple_of(base * LANES, LANES), count * LANES)
        for n in range(num_virt // wide):
            span = slice(n * wide, (n + 1) * wide)
            total = jnp.dot(left, c_all[rows, span], preferred_element_type=jnp.float32)
            if g == 0:
                out_sum[:, span] = total
            else:
                total = total + out_sum[:, span]
                for m in range(2):
                    o_ref[pl.ds(2 * n + m, tile_rows, stride=per_row), :] = total[:, m * LANES:(m + 1) * LANES]

    for copy in to_cross + relay + [to_partner] + h_copies:
        copy.wait_send()
    for p in range(num_pair):
        pl.when(sends(p))(t_copies[p].wait_send)


def shards_kernel(half_ints, coeffs, pair_map, tile_table):
    num_i, sblock, local_j, num_basis = half_ints.shape
    num_virt = coeffs.shape[1]
    num_pair = lax.axis_size("pair")
    local_tiles = num_pair // num_i
    tile_rows = num_virt // local_tiles
    per_row = num_virt // LANES
    num_cols = num_basis // LANES
    ints = half_ints.reshape(num_i, sblock, num_basis)
    bf16 = jnp.bfloat16
    dma = pltpu.SemaphoreType.DMA
    vmem = pl.BlockSpec(memory_space=pltpu.VMEM)
    hbm = pl.BlockSpec(memory_space=pltpu.HBM)
    ints, mine, pair_map, tile_table = (
        pltpu.with_memory_space_constraint(a, pltpu.HBM) for a in (ints, coeffs, pair_map, tile_table))
    out = pl.pallas_call(
        functools.partial(kernel, num_pair, num_i, local_tiles),
        out_shape=jax.ShapeDtypeStruct((tile_rows * per_row, LANES), jnp.float32),
        in_specs=[hbm, hbm, hbm, hbm],
        out_specs=vmem,
        scratch_shapes=[
            pltpu.SMEM(pair_map.shape, jnp.int32),
            pltpu.SMEM(tile_table.shape, jnp.int32),
            pltpu.VMEM((num_basis, num_virt), bf16),
            pltpu.VMEM((local_tiles, tile_rows, num_basis), bf16),
            pltpu.VMEM((num_pair - 1, num_i, sblock, LANES), bf16),
            pltpu.VMEM((num_pair, num_i, sblock, LANES), bf16),
            pltpu.VMEM((num_pair, tile_rows, LANES), bf16),
            pltpu.VMEM((num_cols, tile_rows, LANES), bf16),
            pltpu.VMEM((tile_rows, num_virt), jnp.float32),
            dma((num_pair,)), dma((per_row,)), dma((2,)),
            dma((per_row,)), dma((per_row,)), dma((per_row,)), dma((per_row,)),
            dma, dma,
            dma((num_pair - 1,)), dma((num_pair,)), dma((num_pair,)), dma((num_cols,)),
        ],
        compiler_params=pltpu.CompilerParams(
            collective_id=0, has_side_effects=True, vmem_limit_bytes=40 * 1024 * 1024),
    )(pair_map, tile_table, ints, mine)
    return out.reshape(tile_rows, local_j, num_virt)


def shards(half_ints, coeffs, pair_map, tile_table):
    num_i, sblock, local_j, num_basis = half_ints.shape
    num_virt = coeffs.shape[1]
    num_pair = lax.axis_size("pair")
    fits = (
        num_i == 2 and local_j == 1 and lax.axis_size("occ") == 4 and num_pair == 8
        and sblock % 16 == 0 and sblock * num_pair == num_basis and num_basis == 7 * LANES
        and coeffs.shape[0] * 4 == num_basis and coeffs.shape[0] % 16 == 0
        and num_virt % (2 * LANES) == 0 and num_virt >= 4 * LANES and num_virt % (16 * (num_pair // num_i)) == 0
    )
    body = shards_kernel if fits else shards_general
    return body(half_ints, coeffs, pair_map, tile_table)


def solution(mesh):
    placed = (P(None, "pair", "occ", None), P("occ", None), P(), P())
    return jax.shard_map(
        shards, mesh=mesh, in_specs=placed, out_specs=P("pair", "occ", None), check_vma=False
    )
```

```python
import functools

import jax
import jax.numpy as jnp
from jax import lax
from jax.experimental import pallas as pl
from jax.experimental.pallas import tpu as pltpu
from jax.sharding import PartitionSpec as P


def shards_general(half_ints, coeffs, pair_map, tile_table):
    num_occ = half_ints.shape[0]
    sblock = half_ints.shape[1]
    local_j = half_ints.shape[2]
    num_basis = half_ints.shape[3]
    num_virt = coeffs.shape[1]
    num_pair = lax.axis_size("pair")
    tile_rows = num_occ * num_virt // num_pair
    all_coeffs = lax.all_gather(coeffs, "occ", axis=0, tiled=True)
    flat_ints = half_ints.reshape(num_occ * sblock * local_j, num_basis)
    half_mo = jnp.dot(flat_ints, all_coeffs, preferred_element_type=jnp.float32).astype(
        jnp.bfloat16
    )
    tile_id = jnp.sum(
        jnp.where(jnp.arange(num_pair) == lax.axis_index("pair"), tile_table, 0)
    )
    virt_start = tile_id * tile_rows % num_virt
    column_coeffs = lax.dynamic_slice_in_dim(all_coeffs, virt_start, tile_rows, 1)
    half_flat = half_mo.reshape(num_occ, sblock, local_j * num_virt)
    slot_occ = (tile_table * tile_rows // num_virt)[:, None, None]
    outgoing = jnp.broadcast_to(half_flat[:1], (num_pair,) + half_flat.shape[1:])
    for i in range(1, num_occ):
        outgoing = jnp.where(slot_occ == i, half_flat[i:i + 1], outgoing)
    incoming = lax.all_to_all(outgoing, "pair", split_axis=0, concat_axis=0, tiled=True)
    chosen = (pair_map[:, None] == jnp.arange(num_pair)[None, :]).astype(jnp.bfloat16)
    block_coeffs = jnp.einsum(
        "pg,gsa->psa", chosen, column_coeffs.reshape(num_pair, sblock, tile_rows),
        preferred_element_type=jnp.float32,
    ).astype(jnp.bfloat16)
    result = jnp.einsum("psa,psc->ac", block_coeffs, incoming, preferred_element_type=jnp.float32)
    return result.reshape(tile_rows, local_j, num_virt)


LANES = 128


def kernel(
    num_pair, num_i, local_tiles,
    pm_hbm, tt_hbm, h_hbm, c_hbm, o_ref,
    pm_ref, tt_ref, c_all, ct, hs, hr, ts, tr, out_sum,
    h_sem, c_sem, s_sem, x_send, x_recv, y_send, y_recv, f_send, f_recv, p_send, p_recv,
    h_send, h_recv, t_send, t_recv,
):
    me = lax.axis_index("pair")
    occ = lax.axis_index("occ")
    z, y = me // 2, lax.rem(me, 2)
    core = lax.rem(occ, 2)
    num_basis, num_virt = c_all.shape
    crows = c_hbm.shape[0]
    sblock = h_hbm.shape[1]
    tile_rows = num_virt // local_tiles
    per_row = num_virt // LANES
    num_cols = num_basis // LANES
    middle = num_cols // 2
    partner = occ + 1 - 2 * core
    cross = lax.rem(occ + 2, 4)
    MESH = pl.DeviceIdType.MESH

    def column(plane, line):
        place = 2 * lax.rem(plane, 2) + lax.rem(line + core, 2)
        return middle + (2 * (plane // 2) - 1) * place

    mine = column(z, y)
    shared = mine == middle
    far_planes = (lax.rem(z + 2, 4), 3 - z)
    near_plane = z + 1 - 2 * lax.rem(z, 2)
    far = [(plane, line) for line in (1 - y, y) for plane in far_planes]
    near = [(near_plane, 1 - y), (z, 1 - y), (near_plane, y)]
    peers = [(2 * plane + line, column(plane, line)) for plane, line in far + near]

    def remote(source, target, send, recv, where):
        return pltpu.make_async_remote_copy(
            src_ref=source, dst_ref=target, send_sem=send, recv_sem=recv,
            device_id=where, device_id_type=MESH,
        )

    barrier = pltpu.get_barrier_semaphore()
    greeted = [{"occ": partner}, {"occ": cross}] + [{"pair": p} for p, _ in peers]
    for peer in greeted:
        pl.semaphore_signal(barrier, inc=1, device_id=peer, device_id_type=MESH)

    mine_rows = pl.ds(pl.multiple_of(crows * occ, crows), crows)
    cross_rows = pl.ds(pl.multiple_of(crows * cross, crows), crows)

    def cols(m):
        return pl.ds(pl.multiple_of(m * LANES, LANES), LANES)

    lent = per_row // 3
    back = per_row - lent
    given = [back * y + k for k in range(lent)]
    plain = list(range(lent, back))
    taken = [back * (1 - y) + k for k in range(lent)]
    fetched = given + plain
    arriving = fetched + taken

    def h_column(m):
        return h_hbm.at[:, :, cols(m)]

    fetch_c = [
        pltpu.make_async_copy(c_hbm.at[:, cols(m)], c_all.at[mine_rows, cols(m)], c_sem.at[k])
        for k, m in enumerate(arriving)]
    fetch_h = [
        pltpu.make_async_copy(h_column(m), hs.at[n], h_sem.at[n]) for n, (_, m) in enumerate(peers)]
    fetch_own = pltpu.make_async_copy(h_column(mine), hr.at[me], h_sem.at[len(peers)])
    fetch_pm = pltpu.make_async_copy(pm_hbm, pm_ref, s_sem.at[0])
    fetch_tt = pltpu.make_async_copy(tt_hbm, tt_ref, s_sem.at[1])
    for fetch in fetch_h + fetch_c + [fetch_own, fetch_pm, fetch_tt]:
        fetch.start()

    def passed(m, send, recv, where):
        spot = c_all.at[cross_rows, cols(m)]
        return remote(spot, spot, send, recv, where)

    to_cross = []
    for k, m in enumerate(fetched):
        spot = c_all.at[mine_rows, cols(m)]
        to_cross.append(remote(spot, spot, x_send.at[k], x_recv.at[k], {"occ": cross}))
    relay = [passed(m, f_send.at[k], f_recv.at[k], {"occ": partner}) for k, m in enumerate(arriving)]
    lend = [passed(m, y_send.at[k], y_recv.at[k], {"pair": 2 * z + 1 - y}) for k, m in enumerate(given)]
    borrow = [passed(m, y_send.at[k], y_recv.at[k], {"pair": 2 * z + 1 - y}) for k, m in enumerate(taken)]
    block = c_all.at[mine_rows, :]
    to_partner = remote(block, block, p_send, p_recv, {"occ": partner})
    h_copies = [
        remote(hs.at[n], hr.at[me], h_send.at[n], h_recv.at[me], {"pair": p}) for n, (p, _) in enumerate(peers)]
    h_arrivals = [
        remote(hs.at[n], hr.at[p], h_send.at[n], h_recv.at[p], {"pair": p}) for n, (p, _) in enumerate(peers)]
    t_copies = [
        remote(ts.at[p], tr.at[mine], t_send.at[p], t_recv.at[mine], {"pair": jnp.int32(p)}) for p in range(num_pair)]
    t_arrivals = [
        remote(ts.at[p], tr.at[m], t_send.at[p], t_recv.at[m], {"pair": p}) for p, m in peers]

    for fetch in fetch_c + fetch_h:
        fetch.wait()
    pl.semaphore_wait(barrier, len(greeted))
    for copy in to_cross[:lent]:
        copy.start()
    for copy in h_copies[:2]:
        copy.start()
    for copy in to_cross[lent:]:
        copy.start()
    to_partner.start()
    for copy in h_copies[2:]:
        copy.start()

    def turn(m):
        row = m * LANES
        while row < (m + 1) * LANES:
            j, start = row // tile_rows, row % tile_rows
            count = min(tile_rows - start, (m + 1) * LANES - row)
            ct[j, start:start + count, :] = c_all[:, m * LANES:(m + 1) * LANES].T[row - m * LANES:row - m * LANES + count]
            row += count

    for fetch in (fetch_own, fetch_pm, fetch_tt):
        fetch.wait()
    slot = []
    for g in range(num_pair):
        found = 0
        for p in range(1, num_pair):
            found = jnp.where(pm_ref[p] == g, p, found)
        slot.append(found)
    to_partner.wait_recv()

    def turn_edge(here):
        @pl.when(here == 0)
        def _():
            for m in range(lent):
                turn(m)

        @pl.when(here == 1)
        def _():
            for m in range(back, per_row):
                turn(m)

    for k in range(lent):
        to_cross[k].wait_recv()
        lend[k].start()
        relay[k].start()
    for k in range(lent):
        relay[k].wait_recv()
    turn_edge(y)
    for k in range(lent):
        to_cross[lent + k].wait_recv()
        relay[lent + k].start()
        borrow[k].wait_recv()
        relay[back + k].start()
    for k in range(lent):
        relay[lent + k].wait_recv()
        turn(lent + k)
    for k in range(lent):
        relay[back + k].wait_recv()
    turn_edge(1 - y)
    for copy in h_arrivals:
        copy.wait_recv()

    def tile(p):
        t = tt_ref[p]
        i = jnp.where(t >= local_tiles, 1, 0)
        block = jnp.concatenate([hr[slot[g], i] for g in range(num_pair)], axis=0)
        return jnp.dot(ct[t - local_tiles * i], block, preferred_element_type=jnp.float32).astype(jnp.bfloat16)

    def sends(p):
        away = z // 2 != p // (num_pair // 2)
        return jnp.logical_and(me != p, jnp.logical_not(jnp.logical_and(shared, away)))

    for p in range(num_pair):
        @pl.when(sends(p))
        def _():
            ts[p] = tile(p)
            t_copies[p].start()
    tr[mine] = tile(me)

    own_base = (z // 2) * middle
    far_base = (1 - z // 2) * (middle + 1)
    wide = 2 * LANES
    for g, (base, count, arrivals) in enumerate((
            (own_base, middle + 1, range(len(far), len(peers))), (far_base, middle, range(len(far))))):
        for n in arrivals:
            if g == 1:
                pl.when(peers[n][1] != middle)(t_arrivals[n].wait_recv)
            else:
                t_arrivals[n].wait_recv()
        left = jnp.concatenate([tr[base + u] for u in range(count)], axis=1)
        rows = pl.ds(pl.multiple_of(base * LANES, LANES), count * LANES)
        for n in range(num_virt // wide):
            span = slice(n * wide, (n + 1) * wide)
            total = jnp.dot(left, c_all[rows, span], preferred_element_type=jnp.float32)
            if g == 0:
                out_sum[:, span] = total
            else:
                total = total + out_sum[:, span]
                for m in range(2):
                    o_ref[pl.ds(2 * n + m, tile_rows, stride=per_row), :] = total[:, m * LANES:(m + 1) * LANES]

    for copy in to_cross + lend + relay + [to_partner] + h_copies:
        copy.wait_send()
    for p in range(num_pair):
        pl.when(sends(p))(t_copies[p].wait_send)


def shards_kernel(half_ints, coeffs, pair_map, tile_table):
    num_i, sblock, local_j, num_basis = half_ints.shape
    num_virt = coeffs.shape[1]
    num_pair = lax.axis_size("pair")
    local_tiles = num_pair // num_i
    tile_rows = num_virt // local_tiles
    per_row = num_virt // LANES
    num_cols = num_basis // LANES
    ints = half_ints.reshape(num_i, sblock, num_basis)
    bf16 = jnp.bfloat16
    dma = pltpu.SemaphoreType.DMA
    vmem = pl.BlockSpec(memory_space=pltpu.VMEM)
    hbm = pl.BlockSpec(memory_space=pltpu.HBM)
    ints, mine, pair_map, tile_table = (
        pltpu.with_memory_space_constraint(a, pltpu.HBM) for a in (ints, coeffs, pair_map, tile_table))
    out = pl.pallas_call(
        functools.partial(kernel, num_pair, num_i, local_tiles),
        out_shape=jax.ShapeDtypeStruct((tile_rows * per_row, LANES), jnp.float32),
        in_specs=[hbm, hbm, hbm, hbm],
        out_specs=vmem,
        scratch_shapes=[
            pltpu.SMEM(pair_map.shape, jnp.int32),
            pltpu.SMEM(tile_table.shape, jnp.int32),
            pltpu.VMEM((num_basis, num_virt), bf16),
            pltpu.VMEM((local_tiles, tile_rows, num_basis), bf16),
            pltpu.VMEM((num_pair - 1, num_i, sblock, LANES), bf16),
            pltpu.VMEM((num_pair, num_i, sblock, LANES), bf16),
            pltpu.VMEM((num_pair, tile_rows, LANES), bf16),
            pltpu.VMEM((num_cols, tile_rows, LANES), bf16),
            pltpu.VMEM((tile_rows, num_virt), jnp.float32),
            dma((num_pair,)), dma((per_row,)), dma((2,)),
            dma((per_row,)), dma((per_row,)), dma((per_row,)), dma((per_row,)), dma((per_row,)), dma((per_row,)),
            dma, dma,
            dma((num_pair - 1,)), dma((num_pair,)), dma((num_pair,)), dma((num_cols,)),
        ],
        compiler_params=pltpu.CompilerParams(
            collective_id=0, has_side_effects=True, vmem_limit_bytes=40 * 1024 * 1024),
    )(pair_map, tile_table, ints, mine)
    return out.reshape(tile_rows, local_j, num_virt)


def shards(half_ints, coeffs, pair_map, tile_table):
    num_i, sblock, local_j, num_basis = half_ints.shape
    num_virt = coeffs.shape[1]
    num_pair = lax.axis_size("pair")
    fits = (
        num_i == 2 and local_j == 1 and lax.axis_size("occ") == 4 and num_pair == 8
        and sblock % 16 == 0 and sblock * num_pair == num_basis and num_basis == 7 * LANES
        and coeffs.shape[0] * 4 == num_basis and coeffs.shape[0] % 16 == 0
        and num_virt % (6 * LANES) == 0 and num_virt % (16 * (num_pair // num_i)) == 0
    )
    body = shards_kernel if fits else shards_general
    return body(half_ints, coeffs, pair_map, tile_table)


def solution(mesh):
    placed = (P(None, "pair", "occ", None), P("occ", None), P(), P())
    return jax.shard_map(
        shards, mesh=mesh, in_specs=placed, out_specs=P("pair", "occ", None), check_vma=False
    )
```

```python
import functools

import jax
import jax.numpy as jnp
from jax import lax
from jax.experimental import pallas as pl
from jax.experimental.pallas import tpu as pltpu
from jax.sharding import PartitionSpec as P


def shards_general(half_ints, coeffs, pair_map, tile_table):
    num_occ = half_ints.shape[0]
    sblock = half_ints.shape[1]
    local_j = half_ints.shape[2]
    num_basis = half_ints.shape[3]
    num_virt = coeffs.shape[1]
    num_pair = lax.axis_size("pair")
    tile_rows = num_occ * num_virt // num_pair
    all_coeffs = lax.all_gather(coeffs, "occ", axis=0, tiled=True)
    flat_ints = half_ints.reshape(num_occ * sblock * local_j, num_basis)
    half_mo = jnp.dot(flat_ints, all_coeffs, preferred_element_type=jnp.float32).astype(
        jnp.bfloat16
    )
    tile_id = jnp.sum(
        jnp.where(jnp.arange(num_pair) == lax.axis_index("pair"), tile_table, 0)
    )
    virt_start = tile_id * tile_rows % num_virt
    column_coeffs = lax.dynamic_slice_in_dim(all_coeffs, virt_start, tile_rows, 1)
    half_flat = half_mo.reshape(num_occ, sblock, local_j * num_virt)
    slot_occ = (tile_table * tile_rows // num_virt)[:, None, None]
    outgoing = jnp.broadcast_to(half_flat[:1], (num_pair,) + half_flat.shape[1:])
    for i in range(1, num_occ):
        outgoing = jnp.where(slot_occ == i, half_flat[i:i + 1], outgoing)
    incoming = lax.all_to_all(outgoing, "pair", split_axis=0, concat_axis=0, tiled=True)
    chosen = (pair_map[:, None] == jnp.arange(num_pair)[None, :]).astype(jnp.bfloat16)
    block_coeffs = jnp.einsum(
        "pg,gsa->psa", chosen, column_coeffs.reshape(num_pair, sblock, tile_rows),
        preferred_element_type=jnp.float32,
    ).astype(jnp.bfloat16)
    result = jnp.einsum("psa,psc->ac", block_coeffs, incoming, preferred_element_type=jnp.float32)
    return result.reshape(tile_rows, local_j, num_virt)


LANES = 128
ORDER_A = (0, 6, 1, 7, 2, 3, 4, 5)
ORDER_B = (0, 6, 1, 7, 2, 3, 4, 5)


def kernel(
    num_pair, num_i, local_tiles,
    pm_hbm, tt_hbm, h_hbm, c_hbm, o_ref,
    pm_ref, tt_ref, c_all, ct, hs, hr, ts, tr, out_sum,
    h_sem, c_sem, s_sem, x_send, x_recv, y_send, y_recv, f_send, f_recv, p_send, p_recv,
    h_send, h_recv, t_send, t_recv,
):
    me = lax.axis_index("pair")
    occ = lax.axis_index("occ")
    z, y = me // 2, lax.rem(me, 2)
    core = lax.rem(occ, 2)
    num_basis, num_virt = c_all.shape
    crows = c_hbm.shape[0]
    sblock = h_hbm.shape[1]
    tile_rows = num_virt // local_tiles
    per_row = num_virt // LANES
    num_cols = num_basis // LANES
    middle = num_cols // 2
    partner = occ + 1 - 2 * core
    cross = lax.rem(occ + 2, 4)
    MESH = pl.DeviceIdType.MESH

    def column(plane, line):
        place = 2 * lax.rem(plane, 2) + lax.rem(line + core, 2)
        return middle + (2 * (plane // 2) - 1) * place

    mine = column(z, y)
    shared = mine == middle
    far_planes = (lax.rem(z + 2, 4), 3 - z)
    near_plane = z + 1 - 2 * lax.rem(z, 2)
    far = [(plane, line) for line in (1 - y, y) for plane in far_planes]
    near = [(near_plane, 1 - y), (z, 1 - y), (near_plane, y)]
    peers = [(2 * plane + line, column(plane, line)) for plane, line in far + near]

    def remote(source, target, send, recv, where):
        return pltpu.make_async_remote_copy(
            src_ref=source, dst_ref=target, send_sem=send, recv_sem=recv,
            device_id=where, device_id_type=MESH,
        )

    barrier = pltpu.get_barrier_semaphore()
    greeted = [{"occ": partner}, {"occ": cross}] + [{"pair": p} for p, _ in peers]
    for peer in greeted:
        pl.semaphore_signal(barrier, inc=1, device_id=peer, device_id_type=MESH)

    mine_rows = pl.ds(pl.multiple_of(crows * occ, crows), crows)
    cross_rows = pl.ds(pl.multiple_of(crows * cross, crows), crows)

    def cols(m):
        return pl.ds(pl.multiple_of(m * LANES, LANES), LANES)

    lent = per_row // 3
    back = per_row - lent
    given = [back * y + k for k in range(lent)]
    plain = list(range(lent, back))
    taken = [back * (1 - y) + k for k in range(lent)]
    fetched = given + plain
    arriving = fetched + taken

    def h_column(m):
        return h_hbm.at[:, :, cols(m)]

    fetch_c = [
        pltpu.make_async_copy(c_hbm.at[:, cols(m)], c_all.at[mine_rows, cols(m)], c_sem.at[k])
        for k, m in enumerate(arriving)]
    fetch_h = [
        pltpu.make_async_copy(h_column(m), hs.at[n], h_sem.at[n]) for n, (_, m) in enumerate(peers)]
    fetch_own = pltpu.make_async_copy(h_column(mine), hr.at[me], h_sem.at[len(peers)])
    fetch_pm = pltpu.make_async_copy(pm_hbm, pm_ref, s_sem.at[0])
    fetch_tt = pltpu.make_async_copy(tt_hbm, tt_ref, s_sem.at[1])
    for fetch in fetch_h + fetch_c + [fetch_own, fetch_pm, fetch_tt]:
        fetch.start()

    def passed(m, send, recv, where):
        spot = c_all.at[cross_rows, cols(m)]
        return remote(spot, spot, send, recv, where)

    to_cross = []
    for k, m in enumerate(fetched):
        spot = c_all.at[mine_rows, cols(m)]
        to_cross.append(remote(spot, spot, x_send.at[k], x_recv.at[k], {"occ": cross}))
    relay = [passed(m, f_send.at[k], f_recv.at[k], {"occ": partner}) for k, m in enumerate(arriving)]
    lend = [passed(m, y_send.at[k], y_recv.at[k], {"pair": 2 * z + 1 - y}) for k, m in enumerate(given)]
    borrow = [passed(m, y_send.at[k], y_recv.at[k], {"pair": 2 * z + 1 - y}) for k, m in enumerate(taken)]
    block = c_all.at[mine_rows, :]
    to_partner = remote(block, block, p_send, p_recv, {"occ": partner})
    h_copies = [
        remote(hs.at[n], hr.at[me], h_send.at[n], h_recv.at[me], {"pair": p}) for n, (p, _) in enumerate(peers)]
    h_arrivals = [
        remote(hs.at[n], hr.at[p], h_send.at[n], h_recv.at[p], {"pair": p}) for n, (p, _) in enumerate(peers)]

    served = [a + (b - a) * (z // 2) for a, b in zip(ORDER_A, ORDER_B)]

    def t_copy(p):
        return remote(ts.at[p], tr.at[mine], t_send.at[p], t_recv.at[mine], {"pair": p})

    def t_arrival(m):
        return remote(ts.at[0], tr.at[m], t_send.at[0], t_recv.at[m], {"pair": me})

    for fetch in fetch_c + fetch_h:
        fetch.wait()
    pl.semaphore_wait(barrier, len(greeted))
    for copy in to_cross[:lent]:
        copy.start()
    for copy in h_copies[:2]:
        copy.start()
    for copy in to_cross[lent:]:
        copy.start()
    to_partner.start()
    for copy in h_copies[2:]:
        copy.start()

    def turn(m):
        row = m * LANES
        while row < (m + 1) * LANES:
            j, start = row // tile_rows, row % tile_rows
            count = min(tile_rows - start, (m + 1) * LANES - row)
            ct[j, start:start + count, :] = c_all[:, m * LANES:(m + 1) * LANES].T[row - m * LANES:row - m * LANES + count]
            row += count

    for fetch in (fetch_own, fetch_pm, fetch_tt):
        fetch.wait()
    slot = []
    for g in range(num_pair):
        found = 0
        for p in range(1, num_pair):
            found = jnp.where(pm_ref[p] == g, p, found)
        slot.append(found)
    to_partner.wait_recv()

    def turn_edge(here):
        @pl.when(here == 0)
        def _():
            for m in range(lent):
                turn(m)

        @pl.when(here == 1)
        def _():
            for m in range(back, per_row):
                turn(m)

    for k in range(lent):
        to_cross[k].wait_recv()
        lend[k].start()
        relay[k].start()
    for k in range(lent):
        relay[k].wait_recv()
    turn_edge(y)
    for k in range(lent):
        to_cross[lent + k].wait_recv()
        relay[lent + k].start()
        borrow[k].wait_recv()
        relay[back + k].start()
    for k in range(lent):
        relay[lent + k].wait_recv()
        turn(lent + k)
    for k in range(lent):
        relay[back + k].wait_recv()
    turn_edge(1 - y)
    for copy in h_arrivals:
        copy.wait_recv()

    def tile(p):
        t = tt_ref[p]
        i = jnp.where(t >= local_tiles, 1, 0)
        block = jnp.concatenate([hr[slot[g], i] for g in range(num_pair)], axis=0)
        return jnp.dot(ct[t - local_tiles * i], block, preferred_element_type=jnp.float32).astype(jnp.bfloat16)

    def sends(p):
        away = z // 2 != p // (num_pair // 2)
        return jnp.logical_and(me != p, jnp.logical_not(jnp.logical_and(shared, away)))

    for p in served:
        @pl.when(sends(p))
        def _():
            ts[p] = tile(p)
            t_copy(p).start()
    tr[mine] = tile(me)

    own_base = (z // 2) * middle
    far_base = (1 - z // 2) * (middle + 1)
    wide = 2 * LANES
    parts = ((own_base, middle + 1), (far_base, middle - 1), (far_base + middle - 1, 1))
    for g, (base, count) in enumerate(parts):
        for u in range(count):
            if g == 0:
                pl.when(base + u != mine)(t_arrival(base + u).wait_recv)
            else:
                t_arrival(base + u).wait_recv()
        block = jnp.concatenate([tr[base + u] for u in range(count)], axis=1)
        rows = pl.ds(pl.multiple_of(base * LANES, LANES), count * LANES)
        for n in range(num_virt // wide):
            span = slice(n * wide, (n + 1) * wide)
            total = jnp.dot(block, c_all[rows, span], preferred_element_type=jnp.float32)
            if g > 0:
                total = total + out_sum[:, span]
            if g < len(parts) - 1:
                out_sum[:, span] = total
            else:
                for m in range(2):
                    o_ref[pl.ds(2 * n + m, tile_rows, stride=per_row), :] = total[:, m * LANES:(m + 1) * LANES]

    for copy in to_cross + lend + relay + [to_partner] + h_copies:
        copy.wait_send()
    for p in served:
        pl.when(sends(p))(t_copy(p).wait_send)


def shards_kernel(half_ints, coeffs, pair_map, tile_table):
    num_i, sblock, local_j, num_basis = half_ints.shape
    num_virt = coeffs.shape[1]
    num_pair = lax.axis_size("pair")
    local_tiles = num_pair // num_i
    tile_rows = num_virt // local_tiles
    per_row = num_virt // LANES
    num_cols = num_basis // LANES
    ints = half_ints.reshape(num_i, sblock, num_basis)
    bf16 = jnp.bfloat16
    dma = pltpu.SemaphoreType.DMA
    vmem = pl.BlockSpec(memory_space=pltpu.VMEM)
    hbm = pl.BlockSpec(memory_space=pltpu.HBM)
    ints, mine, pair_map, tile_table = (
        pltpu.with_memory_space_constraint(a, pltpu.HBM) for a in (ints, coeffs, pair_map, tile_table))
    out = pl.pallas_call(
        functools.partial(kernel, num_pair, num_i, local_tiles),
        out_shape=jax.ShapeDtypeStruct((tile_rows * per_row, LANES), jnp.float32),
        in_specs=[hbm, hbm, hbm, hbm],
        out_specs=vmem,
        scratch_shapes=[
            pltpu.SMEM(pair_map.shape, jnp.int32),
            pltpu.SMEM(tile_table.shape, jnp.int32),
            pltpu.VMEM((num_basis, num_virt), bf16),
            pltpu.VMEM((local_tiles, tile_rows, num_basis), bf16),
            pltpu.VMEM((num_pair - 1, num_i, sblock, LANES), bf16),
            pltpu.VMEM((num_pair, num_i, sblock, LANES), bf16),
            pltpu.VMEM((num_pair, tile_rows, LANES), bf16),
            pltpu.VMEM((num_cols, tile_rows, LANES), bf16),
            pltpu.VMEM((tile_rows, num_virt), jnp.float32),
            dma((num_pair,)), dma((per_row,)), dma((2,)),
            dma((per_row,)), dma((per_row,)), dma((per_row,)), dma((per_row,)), dma((per_row,)), dma((per_row,)),
            dma, dma,
            dma((num_pair - 1,)), dma((num_pair,)), dma((num_pair,)), dma((num_cols,)),
        ],
        compiler_params=pltpu.CompilerParams(
            collective_id=0, has_side_effects=True, vmem_limit_bytes=40 * 1024 * 1024),
    )(pair_map, tile_table, ints, mine)
    return out.reshape(tile_rows, local_j, num_virt)


def shards(half_ints, coeffs, pair_map, tile_table):
    num_i, sblock, local_j, num_basis = half_ints.shape
    num_virt = coeffs.shape[1]
    num_pair = lax.axis_size("pair")
    fits = (
        num_i == 2 and local_j == 1 and lax.axis_size("occ") == 4 and num_pair == 8
        and sblock % 16 == 0 and sblock * num_pair == num_basis and num_basis == 7 * LANES
        and coeffs.shape[0] * 4 == num_basis and coeffs.shape[0] % 16 == 0
        and num_virt % (6 * LANES) == 0 and num_virt % (16 * (num_pair // num_i)) == 0
    )
    body = shards_kernel if fits else shards_general
    return body(half_ints, coeffs, pair_map, tile_table)


def solution(mesh):
    placed = (P(None, "pair", "occ", None), P("occ", None), P(), P())
    return jax.shard_map(
        shards, mesh=mesh, in_specs=placed, out_specs=P("pair", "occ", None), check_vma=False
    )
```

```python
import functools

import jax
import jax.numpy as jnp
from jax import lax
from jax.experimental import pallas as pl
from jax.experimental.pallas import tpu as pltpu
from jax.sharding import PartitionSpec as P


def shards_general(half_ints, coeffs, pair_map, tile_table):
    num_occ = half_ints.shape[0]
    sblock = half_ints.shape[1]
    local_j = half_ints.shape[2]
    num_basis = half_ints.shape[3]
    num_virt = coeffs.shape[1]
    num_pair = lax.axis_size("pair")
    tile_rows = num_occ * num_virt // num_pair
    all_coeffs = lax.all_gather(coeffs, "occ", axis=0, tiled=True)
    flat_ints = half_ints.reshape(num_occ * sblock * local_j, num_basis)
    half_mo = jnp.dot(flat_ints, all_coeffs, preferred_element_type=jnp.float32).astype(
        jnp.bfloat16
    )
    tile_id = jnp.sum(
        jnp.where(jnp.arange(num_pair) == lax.axis_index("pair"), tile_table, 0)
    )
    virt_start = tile_id * tile_rows % num_virt
    column_coeffs = lax.dynamic_slice_in_dim(all_coeffs, virt_start, tile_rows, 1)
    half_flat = half_mo.reshape(num_occ, sblock, local_j * num_virt)
    slot_occ = (tile_table * tile_rows // num_virt)[:, None, None]
    outgoing = jnp.broadcast_to(half_flat[:1], (num_pair,) + half_flat.shape[1:])
    for i in range(1, num_occ):
        outgoing = jnp.where(slot_occ == i, half_flat[i:i + 1], outgoing)
    incoming = lax.all_to_all(outgoing, "pair", split_axis=0, concat_axis=0, tiled=True)
    chosen = (pair_map[:, None] == jnp.arange(num_pair)[None, :]).astype(jnp.bfloat16)
    block_coeffs = jnp.einsum(
        "pg,gsa->psa", chosen, column_coeffs.reshape(num_pair, sblock, tile_rows),
        preferred_element_type=jnp.float32,
    ).astype(jnp.bfloat16)
    result = jnp.einsum("psa,psc->ac", block_coeffs, incoming, preferred_element_type=jnp.float32)
    return result.reshape(tile_rows, local_j, num_virt)


LANES = 128
ORDER_A = (0, 6, 1, 7, 2, 3, 4, 5)
ORDER_B = (0, 6, 1, 7, 2, 3, 4, 5)


def kernel(
    num_pair, num_i, local_tiles,
    pm_hbm, tt_hbm, h_hbm, c_hbm, o_ref,
    pm_ref, tt_ref, c_all, ct, hs, hr, ts, tr, out_sum,
    h_sem, c_sem, s_sem, x_send, x_recv, y_send, y_recv, f_send, f_recv, p_send, p_recv,
    h_send, h_recv, t_send, t_recv, ready,
):
    me = lax.axis_index("pair")
    occ = lax.axis_index("occ")
    z, y = me // 2, lax.rem(me, 2)
    core = lax.rem(occ, 2)
    num_basis, num_virt = c_all.shape
    crows = c_hbm.shape[0]
    sblock = h_hbm.shape[1]
    tile_rows = num_virt // local_tiles
    per_row = num_virt // LANES
    num_cols = num_basis // LANES
    middle = num_cols // 2
    partner = occ + 1 - 2 * core
    cross = lax.rem(occ + 2, 4)
    MESH = pl.DeviceIdType.MESH

    def column(plane, line):
        place = 2 * lax.rem(plane, 2) + lax.rem(line + core, 2)
        return middle + (2 * (plane // 2) - 1) * place

    mine = column(z, y)
    shared = mine == middle
    far_planes = (lax.rem(z + 2, 4), 3 - z)
    near_plane = z + 1 - 2 * lax.rem(z, 2)
    far = [(plane, line) for line in (1 - y, y) for plane in far_planes]
    near = [(near_plane, 1 - y), (z, 1 - y), (near_plane, y)]
    peers = [(2 * plane + line, column(plane, line)) for plane, line in far + near]

    def remote(source, target, send, recv, where):
        return pltpu.make_async_remote_copy(
            src_ref=source, dst_ref=target, send_sem=send, recv_sem=recv,
            device_id=where, device_id_type=MESH,
        )

    barrier = pltpu.get_barrier_semaphore()
    inner = lax.rem(z + 1, 4) // 2 == 1
    outer = lax.rem(z + 1, 4) // 2 == 0
    alike = [1, 3, 5]
    unlike = [0, 2, 4, 6]
    greeted = [{"occ": partner}, {"occ": cross}] + [{"pair": peers[n][0]} for n in alike]

    def greet(semaphore, where):
        pl.semaphore_signal(semaphore, inc=1, device_id=where, device_id_type=MESH)

    for peer in greeted:
        greet(barrier, peer)

    @pl.when(inner)
    def _():
        for n in unlike:
            greet(barrier, {"pair": peers[n][0]})

    mine_rows = pl.ds(pl.multiple_of(crows * occ, crows), crows)
    cross_rows = pl.ds(pl.multiple_of(crows * cross, crows), crows)

    def cols(m):
        return pl.ds(pl.multiple_of(m * LANES, LANES), LANES)

    lent = per_row // 3
    back = per_row - lent
    given = [back * y + k for k in range(lent)]
    plain = list(range(lent, back))
    taken = [back * (1 - y) + k for k in range(lent)]
    fetched = given + plain
    arriving = fetched + taken

    def h_column(m):
        return h_hbm.at[:, :, cols(m)]

    fetch_c = [
        pltpu.make_async_copy(c_hbm.at[:, cols(m)], c_all.at[mine_rows, cols(m)], c_sem.at[k])
        for k, m in enumerate(arriving)]
    fetch_h = [
        pltpu.make_async_copy(h_column(m), hs.at[n], h_sem.at[n]) for n, (_, m) in enumerate(peers)]
    fetch_own = pltpu.make_async_copy(h_column(mine), hr.at[me], h_sem.at[len(peers)])
    fetch_pm = pltpu.make_async_copy(pm_hbm, pm_ref, s_sem.at[0])
    fetch_tt = pltpu.make_async_copy(tt_hbm, tt_ref, s_sem.at[1])
    for fetch in fetch_h + fetch_c + [fetch_own, fetch_pm, fetch_tt]:
        fetch.start()

    def passed(m, send, recv, where):
        spot = c_all.at[cross_rows, cols(m)]
        return remote(spot, spot, send, recv, where)

    to_cross = []
    for k, m in enumerate(fetched):
        spot = c_all.at[mine_rows, cols(m)]
        to_cross.append(remote(spot, spot, x_send.at[k], x_recv.at[k], {"occ": cross}))
    relay = [passed(m, f_send.at[k], f_recv.at[k], {"occ": partner}) for k, m in enumerate(arriving)]
    lend = [passed(m, y_send.at[k], y_recv.at[k], {"pair": 2 * z + 1 - y}) for k, m in enumerate(given)]
    borrow = [passed(m, y_send.at[k], y_recv.at[k], {"pair": 2 * z + 1 - y}) for k, m in enumerate(taken)]
    block = c_all.at[mine_rows, :]
    to_partner = remote(block, block, p_send, p_recv, {"occ": partner})
    h_copies = [
        remote(hs.at[n], hr.at[me], h_send.at[n], h_recv.at[me], {"pair": p}) for n, (p, _) in enumerate(peers)]
    h_arrivals = [
        remote(hs.at[n], hr.at[p], h_send.at[n], h_recv.at[p], {"pair": p}) for n, (p, _) in enumerate(peers)]

    served = [a + (b - a) * (z // 2) for a, b in zip(ORDER_A, ORDER_B)]

    def t_copy(p):
        return remote(ts.at[p], tr.at[mine], t_send.at[p], t_recv.at[mine], {"pair": p})

    def t_arrival(m):
        return remote(ts.at[0], tr.at[m], t_send.at[0], t_recv.at[m], {"pair": me})

    for fetch in fetch_c + fetch_h:
        fetch.wait()

    @pl.when(inner)
    def _():
        pl.semaphore_wait(barrier, len(greeted))

    @pl.when(outer)
    def _():
        pl.semaphore_wait(barrier, len(greeted) + len(unlike))
        for n in unlike:
            greet(ready, {"pair": peers[n][0]})

    for copy in to_cross[:lent]:
        copy.start()

    @pl.when(outer)
    def _():
        for copy in h_copies[:2]:
            copy.start()

    @pl.when(inner)
    def _():
        for n in alike:
            h_copies[n].start()

    for copy in to_cross[lent:]:
        copy.start()
    to_partner.start()

    @pl.when(outer)
    def _():
        for copy in h_copies[2:]:
            copy.start()

    @pl.when(inner)
    def _():
        pl.semaphore_wait(ready, len(unlike))
        for n in unlike:
            h_copies[n].start()


    def turn(m):
        row = m * LANES
        while row < (m + 1) * LANES:
            j, start = row // tile_rows, row % tile_rows
            count = min(tile_rows - start, (m + 1) * LANES - row)
            ct[j, start:start + count, :] = c_all[:, m * LANES:(m + 1) * LANES].T[row - m * LANES:row - m * LANES + count]
            row += count

    for fetch in (fetch_own, fetch_pm, fetch_tt):
        fetch.wait()
    slot = []
    for g in range(num_pair):
        found = 0
        for p in range(1, num_pair):
            found = jnp.where(pm_ref[p] == g, p, found)
        slot.append(found)
    to_partner.wait_recv()

    def turn_edge(here):
        @pl.when(here == 0)
        def _():
            for m in range(lent):
                turn(m)

        @pl.when(here == 1)
        def _():
            for m in range(back, per_row):
                turn(m)

    for k in range(lent):
        to_cross[k].wait_recv()
        lend[k].start()
        relay[k].start()
    for k in range(lent):
        relay[k].wait_recv()
    turn_edge(y)
    for k in range(lent):
        to_cross[lent + k].wait_recv()
        relay[lent + k].start()
        borrow[k].wait_recv()
        relay[back + k].start()
    for k in range(lent):
        relay[lent + k].wait_recv()
        turn(lent + k)
    for k in range(lent):
        relay[back + k].wait_recv()
    turn_edge(1 - y)
    for copy in h_arrivals:
        copy.wait_recv()

    def tile(p):
        t = tt_ref[p]
        i = jnp.where(t >= local_tiles, 1, 0)
        block = jnp.concatenate([hr[slot[g], i] for g in range(num_pair)], axis=0)
        return jnp.dot(ct[t - local_tiles * i], block, preferred_element_type=jnp.float32).astype(jnp.bfloat16)

    def sends(p):
        away = z // 2 != p // (num_pair // 2)
        return jnp.logical_and(me != p, jnp.logical_not(jnp.logical_and(shared, away)))

    for p in served:
        @pl.when(sends(p))
        def _():
            ts[p] = tile(p)
            t_copy(p).start()
    tr[mine] = tile(me)

    own_base = (z // 2) * middle
    far_base = (1 - z // 2) * (middle + 1)
    wide = 2 * LANES
    parts = ((own_base, middle + 1), (far_base, middle - 1), (far_base + middle - 1, 1))
    for g, (base, count) in enumerate(parts):
        for u in range(count):
            if g == 0:
                pl.when(base + u != mine)(t_arrival(base + u).wait_recv)
            else:
                t_arrival(base + u).wait_recv()
        block = jnp.concatenate([tr[base + u] for u in range(count)], axis=1)
        rows = pl.ds(pl.multiple_of(base * LANES, LANES), count * LANES)
        for n in range(num_virt // wide):
            span = slice(n * wide, (n + 1) * wide)
            total = jnp.dot(block, c_all[rows, span], preferred_element_type=jnp.float32)
            if g > 0:
                total = total + out_sum[:, span]
            if g < len(parts) - 1:
                out_sum[:, span] = total
            else:
                for m in range(2):
                    o_ref[pl.ds(2 * n + m, tile_rows, stride=per_row), :] = total[:, m * LANES:(m + 1) * LANES]

    for copy in to_cross + lend + relay + [to_partner] + h_copies:
        copy.wait_send()
    for p in served:
        pl.when(sends(p))(t_copy(p).wait_send)


def shards_kernel(half_ints, coeffs, pair_map, tile_table):
    num_i, sblock, local_j, num_basis = half_ints.shape
    num_virt = coeffs.shape[1]
    num_pair = lax.axis_size("pair")
    local_tiles = num_pair // num_i
    tile_rows = num_virt // local_tiles
    per_row = num_virt // LANES
    num_cols = num_basis // LANES
    ints = half_ints.reshape(num_i, sblock, num_basis)
    bf16 = jnp.bfloat16
    dma = pltpu.SemaphoreType.DMA
    vmem = pl.BlockSpec(memory_space=pltpu.VMEM)
    hbm = pl.BlockSpec(memory_space=pltpu.HBM)
    ints, mine, pair_map, tile_table = (
        pltpu.with_memory_space_constraint(a, pltpu.HBM) for a in (ints, coeffs, pair_map, tile_table))
    out = pl.pallas_call(
        functools.partial(kernel, num_pair, num_i, local_tiles),
        out_shape=jax.ShapeDtypeStruct((tile_rows * per_row, LANES), jnp.float32),
        in_specs=[hbm, hbm, hbm, hbm],
        out_specs=vmem,
        scratch_shapes=[
            pltpu.SMEM(pair_map.shape, jnp.int32),
            pltpu.SMEM(tile_table.shape, jnp.int32),
            pltpu.VMEM((num_basis, num_virt), bf16),
            pltpu.VMEM((local_tiles, tile_rows, num_basis), bf16),
            pltpu.VMEM((num_pair - 1, num_i, sblock, LANES), bf16),
            pltpu.VMEM((num_pair, num_i, sblock, LANES), bf16),
            pltpu.VMEM((num_pair, tile_rows, LANES), bf16),
            pltpu.VMEM((num_cols, tile_rows, LANES), bf16),
            pltpu.VMEM((tile_rows, num_virt), jnp.float32),
            dma((num_pair,)), dma((per_row,)), dma((2,)),
            dma((per_row,)), dma((per_row,)), dma((per_row,)), dma((per_row,)), dma((per_row,)), dma((per_row,)),
            dma, dma,
            dma((num_pair - 1,)), dma((num_pair,)), dma((num_pair,)), dma((num_cols,)),
            pltpu.SemaphoreType.REGULAR,
        ],
        compiler_params=pltpu.CompilerParams(
            collective_id=0, has_side_effects=True, vmem_limit_bytes=40 * 1024 * 1024),
    )(pair_map, tile_table, ints, mine)
    return out.reshape(tile_rows, local_j, num_virt)


def shards(half_ints, coeffs, pair_map, tile_table):
    num_i, sblock, local_j, num_basis = half_ints.shape
    num_virt = coeffs.shape[1]
    num_pair = lax.axis_size("pair")
    fits = (
        num_i == 2 and local_j == 1 and lax.axis_size("occ") == 4 and num_pair == 8
        and sblock % 16 == 0 and sblock * num_pair == num_basis and num_basis == 7 * LANES
        and coeffs.shape[0] * 4 == num_basis and coeffs.shape[0] % 16 == 0
        and num_virt % (6 * LANES) == 0 and num_virt % (16 * (num_pair // num_i)) == 0
    )
    body = shards_kernel if fits else shards_general
    return body(half_ints, coeffs, pair_map, tile_table)


def solution(mesh):
    placed = (P(None, "pair", "occ", None), P("occ", None), P(), P())
    return jax.shard_map(
        shards, mesh=mesh, in_specs=placed, out_specs=P("pair", "occ", None), check_vma=False
    )
```

```python
import functools

import jax
import jax.numpy as jnp
from jax import lax
from jax.experimental import pallas as pl
from jax.experimental.pallas import tpu as pltpu
from jax.sharding import PartitionSpec as P


def shards_general(half_ints, coeffs, pair_map, tile_table):
    num_occ = half_ints.shape[0]
    sblock = half_ints.shape[1]
    local_j = half_ints.shape[2]
    num_basis = half_ints.shape[3]
    num_virt = coeffs.shape[1]
    num_pair = lax.axis_size("pair")
    tile_rows = num_occ * num_virt // num_pair
    all_coeffs = lax.all_gather(coeffs, "occ", axis=0, tiled=True)
    flat_ints = half_ints.reshape(num_occ * sblock * local_j, num_basis)
    half_mo = jnp.dot(flat_ints, all_coeffs, preferred_element_type=jnp.float32).astype(
        jnp.bfloat16
    )
    tile_id = jnp.sum(
        jnp.where(jnp.arange(num_pair) == lax.axis_index("pair"), tile_table, 0)
    )
    virt_start = tile_id * tile_rows % num_virt
    column_coeffs = lax.dynamic_slice_in_dim(all_coeffs, virt_start, tile_rows, 1)
    half_flat = half_mo.reshape(num_occ, sblock, local_j * num_virt)
    slot_occ = (tile_table * tile_rows // num_virt)[:, None, None]
    outgoing = jnp.broadcast_to(half_flat[:1], (num_pair,) + half_flat.shape[1:])
    for i in range(1, num_occ):
        outgoing = jnp.where(slot_occ == i, half_flat[i:i + 1], outgoing)
    incoming = lax.all_to_all(outgoing, "pair", split_axis=0, concat_axis=0, tiled=True)
    chosen = (pair_map[:, None] == jnp.arange(num_pair)[None, :]).astype(jnp.bfloat16)
    block_coeffs = jnp.einsum(
        "pg,gsa->psa", chosen, column_coeffs.reshape(num_pair, sblock, tile_rows),
        preferred_element_type=jnp.float32,
    ).astype(jnp.bfloat16)
    result = jnp.einsum("psa,psc->ac", block_coeffs, incoming, preferred_element_type=jnp.float32)
    return result.reshape(tile_rows, local_j, num_virt)


LANES = 128
ORDER_A = (0, 6, 1, 7, 2, 3, 4, 5)
ORDER_B = (0, 6, 1, 7, 2, 3, 4, 5)


def kernel(
    num_pair, num_i, local_tiles,
    pm_hbm, tt_hbm, h_hbm, c_hbm, o_ref,
    pm_ref, tt_ref, c_all, ct, h_all, hs, hr, ts, tr, out_sum,
    h_sem, c_sem, s_sem, x_send, x_recv, y_send, y_recv, f_send, f_recv, p_send, p_recv,
    h_send, h_recv, t_send, t_recv, ready,
):
    me = lax.axis_index("pair")
    occ = lax.axis_index("occ")
    z, y = me // 2, lax.rem(me, 2)
    core = lax.rem(occ, 2)
    num_basis, num_virt = c_all.shape
    crows = c_hbm.shape[0]
    sblock = h_hbm.shape[1]
    tile_rows = num_virt // local_tiles
    per_row = num_virt // LANES
    num_cols = num_basis // LANES
    middle = num_cols // 2
    partner = occ + 1 - 2 * core
    cross = lax.rem(occ + 2, 4)
    MESH = pl.DeviceIdType.MESH

    columns_first = core == 0
    product_first = core == 1

    def column(plane, line):
        place = 2 * lax.rem(plane, 2) + lax.rem(line + core, 2)
        return middle + (2 * (plane // 2) - 1) * place - core * (plane // 2)

    mine = column(z, y)
    shared = 2 * lax.rem(z, 2) + lax.rem(y + core, 2) < 1 + core
    far_planes = (lax.rem(z + 2, 4), 3 - z)
    near_plane = z + 1 - 2 * lax.rem(z, 2)
    far = [(plane, line) for line in (1 - y, y) for plane in far_planes]
    near = [(near_plane, 1 - y), (z, 1 - y), (near_plane, y)]
    peers = [(2 * plane + line, column(plane, line)) for plane, line in far + near]

    def remote(source, target, send, recv, where):
        return pltpu.make_async_remote_copy(
            src_ref=source, dst_ref=target, send_sem=send, recv_sem=recv,
            device_id=where, device_id_type=MESH,
        )

    barrier = pltpu.get_barrier_semaphore()
    inner = lax.rem(z + 1, 4) // 2 == 1
    outer = lax.rem(z + 1, 4) // 2 == 0
    alike = [1, 3, 5]
    unlike = [0, 2, 4, 6]
    greeted = [{"occ": partner}, {"occ": cross}] + [{"pair": peers[n][0]} for n in alike]

    def greet(semaphore, where):
        pl.semaphore_signal(semaphore, inc=1, device_id=where, device_id_type=MESH)

    for peer in greeted:
        greet(barrier, peer)

    @pl.when(inner)
    def _():
        for n in unlike:
            greet(barrier, {"pair": peers[n][0]})

    mine_rows = pl.ds(pl.multiple_of(crows * occ, crows), crows)
    cross_rows = pl.ds(pl.multiple_of(crows * cross, crows), crows)

    def cols(m):
        return pl.ds(pl.multiple_of(m * LANES, LANES), LANES)

    lent = per_row // 3
    back = per_row - lent
    given = [back * y + k for k in range(lent)]
    plain = list(range(lent, back))
    taken = [back * (1 - y) + k for k in range(lent)]
    fetched = given + plain
    arriving = fetched + taken

    def h_column(m):
        return h_hbm.at[:, :, cols(m)]

    fetch_c = [
        pltpu.make_async_copy(c_hbm.at[:, cols(m)], c_all.at[mine_rows, cols(m)], c_sem.at[k])
        for k, m in enumerate(arriving)]
    fetch_h = [
        pltpu.make_async_copy(h_column(m), hs.at[n], h_sem.at[n]) for n, (_, m) in enumerate(peers)]
    fetch_h.append(pltpu.make_async_copy(h_column(mine), hr.at[me], h_sem.at[len(peers)]))
    fetch_all = [
        pltpu.make_async_copy(h_hbm.at[i], h_all.at[pl.ds(i * sblock, sblock), :], h_sem.at[i])
        for i in range(h_hbm.shape[0])]
    fetch_pm = pltpu.make_async_copy(pm_hbm, pm_ref, s_sem.at[0])
    fetch_tt = pltpu.make_async_copy(tt_hbm, tt_ref, s_sem.at[1])
    @pl.when(columns_first)
    def _():
        for fetch in fetch_h:
            fetch.start()

    @pl.when(product_first)
    def _():
        for fetch in fetch_all:
            fetch.start()

    for fetch in fetch_c + [fetch_pm, fetch_tt]:
        fetch.start()

    def passed(m, send, recv, where):
        spot = c_all.at[cross_rows, cols(m)]
        return remote(spot, spot, send, recv, where)

    to_cross = []
    for k, m in enumerate(fetched):
        spot = c_all.at[mine_rows, cols(m)]
        to_cross.append(remote(spot, spot, x_send.at[k], x_recv.at[k], {"occ": cross}))
    relay = [passed(m, f_send.at[k], f_recv.at[k], {"occ": partner}) for k, m in enumerate(arriving)]
    lend = [passed(m, y_send.at[k], y_recv.at[k], {"pair": 2 * z + 1 - y}) for k, m in enumerate(given)]
    borrow = [passed(m, y_send.at[k], y_recv.at[k], {"pair": 2 * z + 1 - y}) for k, m in enumerate(taken)]
    block = c_all.at[mine_rows, :]
    to_partner = remote(block, block, p_send, p_recv, {"occ": partner})
    h_copies = [
        remote(hs.at[n], hr.at[me], h_send.at[p], h_recv.at[me], {"pair": p}) for n, (p, _) in enumerate(peers)]
    h_arrivals = [
        remote(hs.at[n], hr.at[p], h_send.at[p], h_recv.at[p], {"pair": p}) for n, (p, _) in enumerate(peers)]

    served = [a + (b - a) * (z // 2) for a, b in zip(ORDER_A, ORDER_B)]

    def t_copy(p):
        return remote(ts.at[p], tr.at[mine], t_send.at[p], t_recv.at[mine], {"pair": p})

    def t_arrival(m):
        return remote(ts.at[0], tr.at[m], t_send.at[0], t_recv.at[m], {"pair": me})

    for fetch in fetch_c + [fetch_pm, fetch_tt]:
        fetch.wait()

    @pl.when(columns_first)
    def _():
        for fetch in fetch_h:
            fetch.wait()

    @pl.when(product_first)
    def _():
        for fetch in fetch_all:
            fetch.wait()


    @pl.when(inner)
    def _():
        pl.semaphore_wait(barrier, len(greeted))

    @pl.when(outer)
    def _():
        pl.semaphore_wait(barrier, len(greeted) + len(unlike))
        for n in unlike:
            greet(ready, {"pair": peers[n][0]})

    for copy in to_cross[:lent]:
        copy.start()

    @pl.when(jnp.logical_and(outer, columns_first))
    def _():
        for copy in h_copies[:2]:
            copy.start()

    @pl.when(jnp.logical_and(inner, columns_first))
    def _():
        for n in alike:
            h_copies[n].start()

    for copy in to_cross[lent:]:
        copy.start()
    to_partner.start()

    @pl.when(jnp.logical_and(outer, columns_first))
    def _():
        for copy in h_copies[2:]:
            copy.start()

    @pl.when(inner)
    def _():
        pl.semaphore_wait(ready, len(unlike))

    @pl.when(jnp.logical_and(inner, columns_first))
    def _():
        for n in unlike:
            h_copies[n].start()

    def product(m):
        total = jnp.dot(
            h_all[...], c_all[:, m * LANES:(m + 1) * LANES], preferred_element_type=jnp.float32).astype(jnp.bfloat16)
        for i in range(total.shape[0] // sblock):
            hs[m, i] = total[i * sblock:(i + 1) * sblock]
        owners = [(0, middle - m)] if m <= middle else []
        if m >= middle - 1:
            owners.append((2, m - middle + 1))
        for plane, place in owners:
            p = 2 * (plane + place // 2) + lax.rem(place + core, 2)

            @pl.when(p == me)
            def _():
                hr[me] = hs[m]

            @pl.when(p != me)
            def _():
                remote(hs.at[m], hr.at[me], h_send.at[p], h_recv.at[me], {"pair": p}).start()

    def when_product(condition, tiles):
        @pl.when(jnp.logical_and(condition, product_first))
        def _():
            for m in tiles:
                product(m)

    def turn(m):
        row = m * LANES
        while row < (m + 1) * LANES:
            j, start = row // tile_rows, row % tile_rows
            count = min(tile_rows - start, (m + 1) * LANES - row)
            ct[j, start:start + count, :] = c_all[:, m * LANES:(m + 1) * LANES].T[row - m * LANES:row - m * LANES + count]
            row += count

    slot = []
    for g in range(num_pair):
        found = 0
        for p in range(1, num_pair):
            found = jnp.where(pm_ref[p] == g, p, found)
        slot.append(found)
    to_partner.wait_recv()

    def turn_edge(here):
        @pl.when(here == 0)
        def _():
            for m in range(lent):
                turn(m)

        @pl.when(here == 1)
        def _():
            for m in range(back, per_row):
                turn(m)

    for k in range(lent):
        to_cross[k].wait_recv()
        lend[k].start()
        relay[k].start()
    for k in range(lent):
        relay[k].wait_recv()
        when_product(y == 0, [k])
        when_product(y == 1, [back + k])
    turn_edge(y)
    for k in range(lent):
        to_cross[lent + k].wait_recv()
        relay[lent + k].start()
        borrow[k].wait_recv()
        relay[back + k].start()
        relay[lent + k].wait_recv()
        when_product(y < 2, [lent + k])
        relay[back + k].wait_recv()
        when_product(y == 1, [k])
        when_product(y == 0, [back + k])
    for k in range(lent):
        turn(lent + k)
    turn_edge(1 - y)
    for copy in h_arrivals:
        copy.wait_recv()

    def tile(p):
        t = tt_ref[p]
        i = jnp.where(t >= local_tiles, 1, 0)
        block = jnp.concatenate([hr[slot[g], i] for g in range(num_pair)], axis=0)
        return jnp.dot(ct[t - local_tiles * i], block, preferred_element_type=jnp.float32).astype(jnp.bfloat16)

    def sends(p):
        away = z // 2 != p // (num_pair // 2)
        return jnp.logical_and(me != p, jnp.logical_not(jnp.logical_and(shared, away)))

    for p in served:
        @pl.when(sends(p))
        def _():
            ts[p] = tile(p)
            t_copy(p).start()
    tr[mine] = tile(me)

    own_base = (z // 2) * middle
    far_base = (1 - z // 2) * (middle + 1)
    @pl.when(columns_first)
    def _():
        wide = 2 * LANES
        parts = ((own_base, middle + 1), (far_base, middle - 1), (far_base + middle - 1, 1))
        for g, (base, count) in enumerate(parts):
            for u in range(count):
                if g == 0:
                    pl.when(base + u != mine)(t_arrival(base + u).wait_recv)
                else:
                    t_arrival(base + u).wait_recv()
            block = jnp.concatenate([tr[base + u] for u in range(count)], axis=1)
            rows = pl.ds(pl.multiple_of(base * LANES, LANES), count * LANES)
            for n in range(num_virt // wide):
                span = slice(n * wide, (n + 1) * wide)
                total = jnp.dot(block, c_all[rows, span], preferred_element_type=jnp.float32)
                if g > 0:
                    total = total + out_sum[:, span]
                if g < len(parts) - 1:
                    out_sum[:, span] = total
                else:
                    for m in range(2):
                        o_ref[pl.ds(2 * n + m, tile_rows, stride=per_row), :] = total[:, m * LANES:(m + 1) * LANES]

    @pl.when(product_first)
    def _():
        for m in range(per_row):
            pl.when(mine != m)(t_arrival(m).wait_recv)
            o_ref[pl.ds(m, tile_rows, stride=per_row), :] = tr[m].astype(jnp.float32)

    for copy in to_cross + lend + relay + [to_partner] + h_copies:
        copy.wait_send()
    for p in served:
        pl.when(sends(p))(t_copy(p).wait_send)


def shards_kernel(half_ints, coeffs, pair_map, tile_table):
    num_i, sblock, local_j, num_basis = half_ints.shape
    num_virt = coeffs.shape[1]
    num_pair = lax.axis_size("pair")
    local_tiles = num_pair // num_i
    tile_rows = num_virt // local_tiles
    per_row = num_virt // LANES
    num_cols = num_basis // LANES
    ints = half_ints.reshape(num_i, sblock, num_basis)
    bf16 = jnp.bfloat16
    dma = pltpu.SemaphoreType.DMA
    vmem = pl.BlockSpec(memory_space=pltpu.VMEM)
    hbm = pl.BlockSpec(memory_space=pltpu.HBM)
    ints, mine, pair_map, tile_table = (
        pltpu.with_memory_space_constraint(a, pltpu.HBM) for a in (ints, coeffs, pair_map, tile_table))
    out = pl.pallas_call(
        functools.partial(kernel, num_pair, num_i, local_tiles),
        out_shape=jax.ShapeDtypeStruct((tile_rows * per_row, LANES), jnp.float32),
        in_specs=[hbm, hbm, hbm, hbm],
        out_specs=vmem,
        scratch_shapes=[
            pltpu.SMEM(pair_map.shape, jnp.int32),
            pltpu.SMEM(tile_table.shape, jnp.int32),
            pltpu.VMEM((num_basis, num_virt), bf16),
            pltpu.VMEM((local_tiles, tile_rows, num_basis), bf16),
            pltpu.VMEM((num_i * sblock, num_basis), bf16),
            pltpu.VMEM((num_pair - 1, num_i, sblock, LANES), bf16),
            pltpu.VMEM((num_pair, num_i, sblock, LANES), bf16),
            pltpu.VMEM((num_pair, tile_rows, LANES), bf16),
            pltpu.VMEM((num_cols, tile_rows, LANES), bf16),
            pltpu.VMEM((tile_rows, num_virt), jnp.float32),
            dma((num_pair,)), dma((per_row,)), dma((2,)),
            dma((per_row,)), dma((per_row,)), dma((per_row,)), dma((per_row,)), dma((per_row,)), dma((per_row,)),
            dma, dma,
            dma((num_pair,)), dma((num_pair,)), dma((num_pair,)), dma((num_cols,)),
            pltpu.SemaphoreType.REGULAR,
        ],
        compiler_params=pltpu.CompilerParams(
            collective_id=0, has_side_effects=True, vmem_limit_bytes=40 * 1024 * 1024),
    )(pair_map, tile_table, ints, mine)
    return out.reshape(tile_rows, local_j, num_virt)


def shards(half_ints, coeffs, pair_map, tile_table):
    num_i, sblock, local_j, num_basis = half_ints.shape
    num_virt = coeffs.shape[1]
    num_pair = lax.axis_size("pair")
    fits = (
        num_i == 2 and local_j == 1 and lax.axis_size("occ") == 4 and num_pair == 8
        and sblock % 16 == 0 and sblock * num_pair == num_basis and num_basis == 7 * LANES
        and coeffs.shape[0] * 4 == num_basis and coeffs.shape[0] % 16 == 0
        and num_virt == 6 * LANES and num_virt % (16 * (num_pair // num_i)) == 0
    )
    body = shards_kernel if fits else shards_general
    return body(half_ints, coeffs, pair_map, tile_table)


def solution(mesh):
    placed = (P(None, "pair", "occ", None), P("occ", None), P(), P())
    return jax.shard_map(
        shards, mesh=mesh, in_specs=placed, out_specs=P("pair", "occ", None), check_vma=False
    )
```

```python
import functools

import jax
import jax.numpy as jnp
from jax import lax
from jax.experimental import pallas as pl
from jax.experimental.pallas import tpu as pltpu
from jax.sharding import PartitionSpec as P


def shards_general(half_ints, coeffs, pair_map, tile_table):
    num_occ = half_ints.shape[0]
    sblock = half_ints.shape[1]
    local_j = half_ints.shape[2]
    num_basis = half_ints.shape[3]
    num_virt = coeffs.shape[1]
    num_pair = lax.axis_size("pair")
    tile_rows = num_occ * num_virt // num_pair
    all_coeffs = lax.all_gather(coeffs, "occ", axis=0, tiled=True)
    flat_ints = half_ints.reshape(num_occ * sblock * local_j, num_basis)
    half_mo = jnp.dot(flat_ints, all_coeffs, preferred_element_type=jnp.float32).astype(
        jnp.bfloat16
    )
    tile_id = jnp.sum(
        jnp.where(jnp.arange(num_pair) == lax.axis_index("pair"), tile_table, 0)
    )
    virt_start = tile_id * tile_rows % num_virt
    column_coeffs = lax.dynamic_slice_in_dim(all_coeffs, virt_start, tile_rows, 1)
    half_flat = half_mo.reshape(num_occ, sblock, local_j * num_virt)
    slot_occ = (tile_table * tile_rows // num_virt)[:, None, None]
    outgoing = jnp.broadcast_to(half_flat[:1], (num_pair,) + half_flat.shape[1:])
    for i in range(1, num_occ):
        outgoing = jnp.where(slot_occ == i, half_flat[i:i + 1], outgoing)
    incoming = lax.all_to_all(outgoing, "pair", split_axis=0, concat_axis=0, tiled=True)
    chosen = (pair_map[:, None] == jnp.arange(num_pair)[None, :]).astype(jnp.bfloat16)
    block_coeffs = jnp.einsum(
        "pg,gsa->psa", chosen, column_coeffs.reshape(num_pair, sblock, tile_rows),
        preferred_element_type=jnp.float32,
    ).astype(jnp.bfloat16)
    result = jnp.einsum("psa,psc->ac", block_coeffs, incoming, preferred_element_type=jnp.float32)
    return result.reshape(tile_rows, local_j, num_virt)


LANES = 128
ORDER_A = (0, 6, 1, 7, 2, 3, 4, 5)
ORDER_B = (0, 6, 1, 7, 2, 3, 4, 5)


def kernel(
    num_pair, num_i, local_tiles,
    pm_hbm, tt_hbm, h_hbm, c_hbm, o_ref,
    pm_ref, tt_ref, c_all, ct, hs, hr, ts, tr, out_sum,
    h_sem, c_sem, s_sem, x_send, x_recv, y_send, y_recv, f_send, f_recv, p_send, p_recv,
    h_send, h_recv, t_send, t_recv, ready,
):
    me = lax.axis_index("pair")
    occ = lax.axis_index("occ")
    z, y = me // 2, lax.rem(me, 2)
    core = lax.rem(occ, 2)
    num_basis, num_virt = c_all.shape
    crows = c_hbm.shape[0]
    sblock = h_hbm.shape[1]
    tile_rows = num_virt // local_tiles
    per_row = num_virt // LANES
    num_cols = num_basis // LANES
    middle = num_cols // 2
    partner = occ + 1 - 2 * core
    cross = lax.rem(occ + 2, 4)
    MESH = pl.DeviceIdType.MESH

    def column(plane, line):
        place = 2 * (lax.rem(plane + 1, 4) // 2) + lax.rem(line + core, 2)
        return middle + (2 * (plane // 2) - 1) * place

    mine = column(z, y)
    shared = mine == middle
    far_planes = (lax.rem(z + 2, 4), 3 - z)
    near_plane = z + 1 - 2 * lax.rem(z, 2)
    far = [(plane, line) for line in (1 - y, y) for plane in far_planes]
    near = [(near_plane, 1 - y), (z, 1 - y), (near_plane, y)]
    peers = [(2 * plane + line, column(plane, line)) for plane, line in far + near]

    def remote(source, target, send, recv, where):
        return pltpu.make_async_remote_copy(
            src_ref=source, dst_ref=target, send_sem=send, recv_sem=recv,
            device_id=where, device_id_type=MESH,
        )

    barrier = pltpu.get_barrier_semaphore()
    inner = lax.rem(z + 1, 4) // 2 == 1
    outer = lax.rem(z + 1, 4) // 2 == 0
    alike = [1, 3, 5]
    unlike = [0, 2, 4, 6]
    greeted = [{"occ": partner}, {"occ": cross}] + [{"pair": peers[n][0]} for n in alike]

    def greet(semaphore, where):
        pl.semaphore_signal(semaphore, inc=1, device_id=where, device_id_type=MESH)

    for peer in greeted:
        greet(barrier, peer)

    @pl.when(inner)
    def _():
        for n in unlike:
            greet(barrier, {"pair": peers[n][0]})

    mine_rows = pl.ds(pl.multiple_of(crows * occ, crows), crows)
    cross_rows = pl.ds(pl.multiple_of(crows * cross, crows), crows)

    def cols(m):
        return pl.ds(pl.multiple_of(m * LANES, LANES), LANES)

    lent = per_row // 3
    back = per_row - lent
    given = [back * y + k for k in range(lent)]
    plain = list(range(lent, back))
    taken = [back * (1 - y) + k for k in range(lent)]
    fetched = given + plain
    arriving = fetched + taken

    def h_column(m):
        return h_hbm.at[:, :, cols(m)]

    fetch_c = [
        pltpu.make_async_copy(c_hbm.at[:, cols(m)], c_all.at[mine_rows, cols(m)], c_sem.at[k])
        for k, m in enumerate(arriving)]
    fetch_h = [
        pltpu.make_async_copy(h_column(m), hs.at[n], h_sem.at[n]) for n, (_, m) in enumerate(peers)]
    fetch_own = pltpu.make_async_copy(h_column(mine), hr.at[me], h_sem.at[len(peers)])
    fetch_pm = pltpu.make_async_copy(pm_hbm, pm_ref, s_sem.at[0])
    fetch_tt = pltpu.make_async_copy(tt_hbm, tt_ref, s_sem.at[1])
    for fetch in fetch_h + fetch_c + [fetch_own, fetch_pm, fetch_tt]:
        fetch.start()

    def passed(m, send, recv, where):
        spot = c_all.at[cross_rows, cols(m)]
        return remote(spot, spot, send, recv, where)

    to_cross = []
    for k, m in enumerate(fetched):
        spot = c_all.at[mine_rows, cols(m)]
        to_cross.append(remote(spot, spot, x_send.at[k], x_recv.at[k], {"occ": cross}))
    relay = [passed(m, f_send.at[k], f_recv.at[k], {"occ": partner}) for k, m in enumerate(arriving)]
    lend = [passed(m, y_send.at[k], y_recv.at[k], {"pair": 2 * z + 1 - y}) for k, m in enumerate(given)]
    borrow = [passed(m, y_send.at[k], y_recv.at[k], {"pair": 2 * z + 1 - y}) for k, m in enumerate(taken)]
    block = c_all.at[mine_rows, :]
    to_partner = remote(block, block, p_send, p_recv, {"occ": partner})
    h_copies = [
        remote(hs.at[n], hr.at[me], h_send.at[n], h_recv.at[me], {"pair": p}) for n, (p, _) in enumerate(peers)]
    h_arrivals = [
        remote(hs.at[n], hr.at[p], h_send.at[n], h_recv.at[p], {"pair": p}) for n, (p, _) in enumerate(peers)]

    served = [a + (b - a) * (z // 2) for a, b in zip(ORDER_A, ORDER_B)]

    def t_copy(p):
        return remote(ts.at[p], tr.at[mine], t_send.at[p], t_recv.at[mine], {"pair": p})

    def t_arrival(m):
        return remote(ts.at[0], tr.at[m], t_send.at[0], t_recv.at[m], {"pair": me})

    for fetch in fetch_c + fetch_h:
        fetch.wait()

    @pl.when(inner)
    def _():
        pl.semaphore_wait(barrier, len(greeted))

    @pl.when(outer)
    def _():
        pl.semaphore_wait(barrier, len(greeted) + len(unlike))
        for n in unlike:
            greet(ready, {"pair": peers[n][0]})

    for copy in to_cross[:lent]:
        copy.start()

    @pl.when(outer)
    def _():
        for copy in h_copies[:2]:
            copy.start()

    @pl.when(inner)
    def _():
        for n in alike:
            h_copies[n].start()

    for copy in to_cross[lent:]:
        copy.start()
    to_partner.start()

    @pl.when(outer)
    def _():
        for copy in h_copies[2:]:
            copy.start()

    @pl.when(inner)
    def _():
        pl.semaphore_wait(ready, len(unlike))
        for n in unlike:
            h_copies[n].start()


    def turn(m):
        row = m * LANES
        while row < (m + 1) * LANES:
            j, start = row // tile_rows, row % tile_rows
            count = min(tile_rows - start, (m + 1) * LANES - row)
            ct[j, start:start + count, :] = c_all[:, m * LANES:(m + 1) * LANES].T[row - m * LANES:row - m * LANES + count]
            row += count

    for fetch in (fetch_own, fetch_pm, fetch_tt):
        fetch.wait()
    slot = []
    for g in range(num_pair):
        found = 0
        for p in range(1, num_pair):
            found = jnp.where(pm_ref[p] == g, p, found)
        slot.append(found)
    to_partner.wait_recv()

    def turn_edge(here):
        @pl.when(here == 0)
        def _():
            for m in range(lent):
                turn(m)

        @pl.when(here == 1)
        def _():
            for m in range(back, per_row):
                turn(m)

    for k in range(lent):
        to_cross[k].wait_recv()
        lend[k].start()
        relay[k].start()
    for k in range(lent):
        relay[k].wait_recv()
    turn_edge(y)
    for k in range(lent):
        to_cross[lent + k].wait_recv()
        relay[lent + k].start()
        borrow[k].wait_recv()
        relay[back + k].start()
    for k in range(lent):
        relay[lent + k].wait_recv()
        turn(lent + k)
    for k in range(lent):
        relay[back + k].wait_recv()
    turn_edge(1 - y)
    for copy in h_arrivals:
        copy.wait_recv()

    def tile(p):
        t = tt_ref[p]
        i = jnp.where(t >= local_tiles, 1, 0)
        block = jnp.concatenate([hr[slot[g], i] for g in range(num_pair)], axis=0)
        return jnp.dot(ct[t - local_tiles * i], block, preferred_element_type=jnp.float32).astype(jnp.bfloat16)

    def sends(p):
        away = z // 2 != p // (num_pair // 2)
        return jnp.logical_and(me != p, jnp.logical_not(jnp.logical_and(shared, away)))

    for p in served:
        @pl.when(sends(p))
        def _():
            ts[p] = tile(p)
            t_copy(p).start()
    tr[mine] = tile(me)

    own_base = (z // 2) * middle
    far_base = (1 - z // 2) * (middle + 1)
    wide = 2 * LANES
    parts = ((own_base, middle + 1), (far_base, middle - 1), (far_base + middle - 1, 1))
    for g, (base, count) in enumerate(parts):
        for u in range(count):
            if g == 0:
                pl.when(base + u != mine)(t_arrival(base + u).wait_recv)
            else:
                t_arrival(base + u).wait_recv()
        block = jnp.concatenate([tr[base + u] for u in range(count)], axis=1)
        rows = pl.ds(pl.multiple_of(base * LANES, LANES), count * LANES)
        for n in range(num_virt // wide):
            span = slice(n * wide, (n + 1) * wide)
            total = jnp.dot(block, c_all[rows, span], preferred_element_type=jnp.float32)
            if g > 0:
                total = total + out_sum[:, span]
            if g < len(parts) - 1:
                out_sum[:, span] = total
            else:
                for m in range(2):
                    o_ref[pl.ds(2 * n + m, tile_rows, stride=per_row), :] = total[:, m * LANES:(m + 1) * LANES]

    for copy in to_cross + lend + relay + [to_partner] + h_copies:
        copy.wait_send()
    for p in served:
        pl.when(sends(p))(t_copy(p).wait_send)


def shards_kernel(half_ints, coeffs, pair_map, tile_table):
    num_i, sblock, local_j, num_basis = half_ints.shape
    num_virt = coeffs.shape[1]
    num_pair = lax.axis_size("pair")
    local_tiles = num_pair // num_i
    tile_rows = num_virt // local_tiles
    per_row = num_virt // LANES
    num_cols = num_basis // LANES
    ints = half_ints.reshape(num_i, sblock, num_basis)
    bf16 = jnp.bfloat16
    dma = pltpu.SemaphoreType.DMA
    vmem = pl.BlockSpec(memory_space=pltpu.VMEM)
    hbm = pl.BlockSpec(memory_space=pltpu.HBM)
    ints, mine, pair_map, tile_table = (
        pltpu.with_memory_space_constraint(a, pltpu.HBM) for a in (ints, coeffs, pair_map, tile_table))
    out = pl.pallas_call(
        functools.partial(kernel, num_pair, num_i, local_tiles),
        out_shape=jax.ShapeDtypeStruct((tile_rows * per_row, LANES), jnp.float32),
        in_specs=[hbm, hbm, hbm, hbm],
        out_specs=vmem,
        scratch_shapes=[
            pltpu.SMEM(pair_map.shape, jnp.int32),
            pltpu.SMEM(tile_table.shape, jnp.int32),
            pltpu.VMEM((num_basis, num_virt), bf16),
            pltpu.VMEM((local_tiles, tile_rows, num_basis), bf16),
            pltpu.VMEM((num_pair - 1, num_i, sblock, LANES), bf16),
            pltpu.VMEM((num_pair, num_i, sblock, LANES), bf16),
            pltpu.VMEM((num_pair, tile_rows, LANES), bf16),
            pltpu.VMEM((num_cols, tile_rows, LANES), bf16),
            pltpu.VMEM((tile_rows, num_virt), jnp.float32),
            dma((num_pair,)), dma((per_row,)), dma((2,)),
            dma((per_row,)), dma((per_row,)), dma((per_row,)), dma((per_row,)), dma((per_row,)), dma((per_row,)),
            dma, dma,
            dma((num_pair - 1,)), dma((num_pair,)), dma((num_pair,)), dma((num_cols,)),
            pltpu.SemaphoreType.REGULAR,
        ],
        compiler_params=pltpu.CompilerParams(
            collective_id=0, has_side_effects=True, vmem_limit_bytes=40 * 1024 * 1024),
    )(pair_map, tile_table, ints, mine)
    return out.reshape(tile_rows, local_j, num_virt)


def shards(half_ints, coeffs, pair_map, tile_table):
    num_i, sblock, local_j, num_basis = half_ints.shape
    num_virt = coeffs.shape[1]
    num_pair = lax.axis_size("pair")
    fits = (
        num_i == 2 and local_j == 1 and lax.axis_size("occ") == 4 and num_pair == 8
        and sblock % 16 == 0 and sblock * num_pair == num_basis and num_basis == 7 * LANES
        and coeffs.shape[0] * 4 == num_basis and coeffs.shape[0] % 16 == 0
        and num_virt % (6 * LANES) == 0 and num_virt % (16 * (num_pair // num_i)) == 0
    )
    body = shards_kernel if fits else shards_general
    return body(half_ints, coeffs, pair_map, tile_table)


def solution(mesh):
    placed = (P(None, "pair", "occ", None), P("occ", None), P(), P())
    return jax.shard_map(
        shards, mesh=mesh, in_specs=placed, out_specs=P("pair", "occ", None), check_vma=False
    )
```

```python
import functools

import jax
import jax.numpy as jnp
from jax import lax
from jax.experimental import pallas as pl
from jax.experimental.pallas import tpu as pltpu
from jax.sharding import PartitionSpec as P


def shards_general(half_ints, coeffs, pair_map, tile_table):
    num_occ = half_ints.shape[0]
    sblock = half_ints.shape[1]
    local_j = half_ints.shape[2]
    num_basis = half_ints.shape[3]
    num_virt = coeffs.shape[1]
    num_pair = lax.axis_size("pair")
    tile_rows = num_occ * num_virt // num_pair
    all_coeffs = lax.all_gather(coeffs, "occ", axis=0, tiled=True)
    flat_ints = half_ints.reshape(num_occ * sblock * local_j, num_basis)
    half_mo = jnp.dot(flat_ints, all_coeffs, preferred_element_type=jnp.float32).astype(
        jnp.bfloat16
    )
    tile_id = jnp.sum(
        jnp.where(jnp.arange(num_pair) == lax.axis_index("pair"), tile_table, 0)
    )
    virt_start = tile_id * tile_rows % num_virt
    column_coeffs = lax.dynamic_slice_in_dim(all_coeffs, virt_start, tile_rows, 1)
    half_flat = half_mo.reshape(num_occ, sblock, local_j * num_virt)
    slot_occ = (tile_table * tile_rows // num_virt)[:, None, None]
    outgoing = jnp.broadcast_to(half_flat[:1], (num_pair,) + half_flat.shape[1:])
    for i in range(1, num_occ):
        outgoing = jnp.where(slot_occ == i, half_flat[i:i + 1], outgoing)
    incoming = lax.all_to_all(outgoing, "pair", split_axis=0, concat_axis=0, tiled=True)
    chosen = (pair_map[:, None] == jnp.arange(num_pair)[None, :]).astype(jnp.bfloat16)
    block_coeffs = jnp.einsum(
        "pg,gsa->psa", chosen, column_coeffs.reshape(num_pair, sblock, tile_rows),
        preferred_element_type=jnp.float32,
    ).astype(jnp.bfloat16)
    result = jnp.einsum("psa,psc->ac", block_coeffs, incoming, preferred_element_type=jnp.float32)
    return result.reshape(tile_rows, local_j, num_virt)


LANES = 128
ORDER_A = (0, 6, 1, 7, 2, 3, 4, 5)
ORDER_B = (0, 6, 1, 7, 2, 3, 4, 5)


def kernel(
    num_pair, num_i, local_tiles,
    pm_hbm, tt_hbm, h_hbm, c_hbm, o_ref,
    pm_ref, tt_ref, c_all, ct, hs, hr, ts, tr, out_sum,
    h_sem, c_sem, s_sem, x_send, x_recv, y_send, y_recv, f_send, f_recv, p_send, p_recv,
    h_send, h_recv, t_send, t_recv, ready,
):
    me = lax.axis_index("pair")
    occ = lax.axis_index("occ")
    z, y = me // 2, lax.rem(me, 2)
    core = lax.rem(occ, 2)
    num_basis, num_virt = c_all.shape
    crows = c_hbm.shape[0]
    sblock = h_hbm.shape[1]
    tile_rows = num_virt // local_tiles
    per_row = num_virt // LANES
    num_cols = num_basis // LANES
    middle = num_cols // 2
    partner = occ + 1 - 2 * core
    cross = lax.rem(occ + 2, 4)
    MESH = pl.DeviceIdType.MESH

    def column(plane, line):
        place = 2 * (lax.rem(plane + 1, 4) // 2) + lax.rem(line + core, 2)
        return middle + (2 * (plane // 2) - 1) * place

    mine = column(z, y)
    shared = mine == middle
    far_planes = (lax.rem(z + 2, 4), 3 - z)
    near_plane = z + 1 - 2 * lax.rem(z, 2)
    line_a = (lax.rem(z + 1, 4) // 2) * (1 - core) + (1 - (lax.rem(z + 1, 4) // 2)) * (1 - y)
    far = [(plane, line) for line in (line_a, 1 - line_a) for plane in far_planes]
    near = [(near_plane, line_a), (z, 1 - y), (near_plane, 1 - line_a)]
    peers = [(2 * plane + line, column(plane, line)) for plane, line in far + near]

    def remote(source, target, send, recv, where):
        return pltpu.make_async_remote_copy(
            src_ref=source, dst_ref=target, send_sem=send, recv_sem=recv,
            device_id=where, device_id_type=MESH,
        )

    barrier = pltpu.get_barrier_semaphore()
    inner = lax.rem(z + 1, 4) // 2 == 1
    outer = lax.rem(z + 1, 4) // 2 == 0
    alike = [1, 3, 5]
    unlike = [0, 2, 4, 6]
    greeted = [{"occ": partner}, {"occ": cross}] + [{"pair": peers[n][0]} for n in alike]

    def greet(semaphore, where):
        pl.semaphore_signal(semaphore, inc=1, device_id=where, device_id_type=MESH)

    for peer in greeted:
        greet(barrier, peer)

    @pl.when(inner)
    def _():
        for n in unlike:
            greet(barrier, {"pair": peers[n][0]})

    mine_rows = pl.ds(pl.multiple_of(crows * occ, crows), crows)
    cross_rows = pl.ds(pl.multiple_of(crows * cross, crows), crows)

    def cols(m):
        return pl.ds(pl.multiple_of(m * LANES, LANES), LANES)

    lent = per_row // 3
    back = per_row - lent
    given = [back * y + k for k in range(lent)]
    plain = list(range(lent, back))
    taken = [back * (1 - y) + k for k in range(lent)]
    fetched = given + plain
    arriving = fetched + taken

    def h_column(m):
        return h_hbm.at[:, :, cols(m)]

    fetch_c = [
        pltpu.make_async_copy(c_hbm.at[:, cols(m)], c_all.at[mine_rows, cols(m)], c_sem.at[k])
        for k, m in enumerate(arriving)]
    fetch_h = [
        pltpu.make_async_copy(h_column(m), hs.at[n], h_sem.at[n]) for n, (_, m) in enumerate(peers)]
    fetch_own = pltpu.make_async_copy(h_column(mine), hr.at[me], h_sem.at[len(peers)])
    fetch_pm = pltpu.make_async_copy(pm_hbm, pm_ref, s_sem.at[0])
    fetch_tt = pltpu.make_async_copy(tt_hbm, tt_ref, s_sem.at[1])
    for fetch in fetch_h + fetch_c + [fetch_own, fetch_pm, fetch_tt]:
        fetch.start()

    def passed(m, send, recv, where):
        spot = c_all.at[cross_rows, cols(m)]
        return remote(spot, spot, send, recv, where)

    to_cross = []
    for k, m in enumerate(fetched):
        spot = c_all.at[mine_rows, cols(m)]
        to_cross.append(remote(spot, spot, x_send.at[k], x_recv.at[k], {"occ": cross}))
    relay = [passed(m, f_send.at[k], f_recv.at[k], {"occ": partner}) for k, m in enumerate(arriving)]
    lend = [passed(m, y_send.at[k], y_recv.at[k], {"pair": 2 * z + 1 - y}) for k, m in enumerate(given)]
    borrow = [passed(m, y_send.at[k], y_recv.at[k], {"pair": 2 * z + 1 - y}) for k, m in enumerate(taken)]
    block = c_all.at[mine_rows, :]
    to_partner = remote(block, block, p_send, p_recv, {"occ": partner})
    h_copies = [
        remote(hs.at[n], hr.at[me], h_send.at[n], h_recv.at[me], {"pair": p}) for n, (p, _) in enumerate(peers)]
    h_arrivals = [
        remote(hs.at[n], hr.at[p], h_send.at[n], h_recv.at[p], {"pair": p}) for n, (p, _) in enumerate(peers)]

    served = [a + (b - a) * (z // 2) for a, b in zip(ORDER_A, ORDER_B)]

    def t_copy(p):
        return remote(ts.at[p], tr.at[mine], t_send.at[p], t_recv.at[mine], {"pair": p})

    def t_arrival(m):
        return remote(ts.at[0], tr.at[m], t_send.at[0], t_recv.at[m], {"pair": me})

    for fetch in fetch_c + fetch_h:
        fetch.wait()

    @pl.when(inner)
    def _():
        pl.semaphore_wait(barrier, len(greeted))

    @pl.when(outer)
    def _():
        pl.semaphore_wait(barrier, len(greeted) + len(unlike))
        for n in unlike:
            greet(ready, {"pair": peers[n][0]})

    for copy in to_cross[:lent]:
        copy.start()

    @pl.when(outer)
    def _():
        for copy in h_copies[:2]:
            copy.start()

    @pl.when(inner)
    def _():
        for n in alike:
            h_copies[n].start()

    for copy in to_cross[lent:]:
        copy.start()
    to_partner.start()

    @pl.when(outer)
    def _():
        for copy in h_copies[2:]:
            copy.start()

    @pl.when(inner)
    def _():
        pl.semaphore_wait(ready, len(unlike))
        for n in (0, 4, 2, 6):
            h_copies[n].start()


    def turn(m):
        row = m * LANES
        while row < (m + 1) * LANES:
            j, start = row // tile_rows, row % tile_rows
            count = min(tile_rows - start, (m + 1) * LANES - row)
            ct[j, start:start + count, :] = c_all[:, m * LANES:(m + 1) * LANES].T[row - m * LANES:row - m * LANES + count]
            row += count

    for fetch in (fetch_own, fetch_pm, fetch_tt):
        fetch.wait()
    slot = []
    for g in range(num_pair):
        found = 0
        for p in range(1, num_pair):
            found = jnp.where(pm_ref[p] == g, p, found)
        slot.append(found)
    to_partner.wait_recv()

    def turn_edge(here):
        @pl.when(here == 0)
        def _():
            for m in range(lent):
                turn(m)

        @pl.when(here == 1)
        def _():
            for m in range(back, per_row):
                turn(m)

    for k in range(lent):
        to_cross[k].wait_recv()
        lend[k].start()
        relay[k].start()
    for k in range(lent):
        relay[k].wait_recv()
    turn_edge(y)
    for k in range(lent):
        to_cross[lent + k].wait_recv()
        relay[lent + k].start()
        borrow[k].wait_recv()
        relay[back + k].start()
    for k in range(lent):
        relay[lent + k].wait_recv()
        turn(lent + k)
    for k in range(lent):
        relay[back + k].wait_recv()
    turn_edge(1 - y)
    for copy in h_arrivals:
        copy.wait_recv()

    def tile(p):
        t = tt_ref[p]
        i = jnp.where(t >= local_tiles, 1, 0)
        block = jnp.concatenate([hr[slot[g], i] for g in range(num_pair)], axis=0)
        return jnp.dot(ct[t - local_tiles * i], block, preferred_element_type=jnp.float32).astype(jnp.bfloat16)

    def sends(p):
        away = z // 2 != p // (num_pair // 2)
        return jnp.logical_and(me != p, jnp.logical_not(jnp.logical_and(shared, away)))

    for p in served:
        @pl.when(sends(p))
        def _():
            ts[p] = tile(p)
            t_copy(p).start()
    tr[mine] = tile(me)

    own_base = (z // 2) * middle
    far_base = (1 - z // 2) * (middle + 1)
    wide = 2 * LANES
    parts = ((own_base, middle + 1), (far_base, middle - 1), (far_base + middle - 1, 1))
    for g, (base, count) in enumerate(parts):
        for u in range(count):
            if g == 0:
                pl.when(base + u != mine)(t_arrival(base + u).wait_recv)
            else:
                t_arrival(base + u).wait_recv()
        block = jnp.concatenate([tr[base + u] for u in range(count)], axis=1)
        rows = pl.ds(pl.multiple_of(base * LANES, LANES), count * LANES)
        for n in range(num_virt // wide):
            span = slice(n * wide, (n + 1) * wide)
            total = jnp.dot(block, c_all[rows, span], preferred_element_type=jnp.float32)
            if g > 0:
                total = total + out_sum[:, span]
            if g < len(parts) - 1:
                out_sum[:, span] = total
            else:
                for m in range(2):
                    o_ref[pl.ds(2 * n + m, tile_rows, stride=per_row), :] = total[:, m * LANES:(m + 1) * LANES]

    for copy in to_cross + lend + relay + [to_partner] + h_copies:
        copy.wait_send()
    for p in served:
        pl.when(sends(p))(t_copy(p).wait_send)


def shards_kernel(half_ints, coeffs, pair_map, tile_table):
    num_i, sblock, local_j, num_basis = half_ints.shape
    num_virt = coeffs.shape[1]
    num_pair = lax.axis_size("pair")
    local_tiles = num_pair // num_i
    tile_rows = num_virt // local_tiles
    per_row = num_virt // LANES
    num_cols = num_basis // LANES
    ints = half_ints.reshape(num_i, sblock, num_basis)
    bf16 = jnp.bfloat16
    dma = pltpu.SemaphoreType.DMA
    vmem = pl.BlockSpec(memory_space=pltpu.VMEM)
    hbm = pl.BlockSpec(memory_space=pltpu.HBM)
    ints, mine, pair_map, tile_table = (
        pltpu.with_memory_space_constraint(a, pltpu.HBM) for a in (ints, coeffs, pair_map, tile_table))
    out = pl.pallas_call(
        functools.partial(kernel, num_pair, num_i, local_tiles),
        out_shape=jax.ShapeDtypeStruct((tile_rows * per_row, LANES), jnp.float32),
        in_specs=[hbm, hbm, hbm, hbm],
        out_specs=vmem,
        scratch_shapes=[
            pltpu.SMEM(pair_map.shape, jnp.int32),
            pltpu.SMEM(tile_table.shape, jnp.int32),
            pltpu.VMEM((num_basis, num_virt), bf16),
            pltpu.VMEM((local_tiles, tile_rows, num_basis), bf16),
            pltpu.VMEM((num_pair - 1, num_i, sblock, LANES), bf16),
            pltpu.VMEM((num_pair, num_i, sblock, LANES), bf16),
            pltpu.VMEM((num_pair, tile_rows, LANES), bf16),
            pltpu.VMEM((num_cols, tile_rows, LANES), bf16),
            pltpu.VMEM((tile_rows, num_virt), jnp.float32),
            dma((num_pair,)), dma((per_row,)), dma((2,)),
            dma((per_row,)), dma((per_row,)), dma((per_row,)), dma((per_row,)), dma((per_row,)), dma((per_row,)),
            dma, dma,
            dma((num_pair - 1,)), dma((num_pair,)), dma((num_pair,)), dma((num_cols,)),
            pltpu.SemaphoreType.REGULAR,
        ],
        compiler_params=pltpu.CompilerParams(
            collective_id=0, has_side_effects=True, vmem_limit_bytes=40 * 1024 * 1024),
    )(pair_map, tile_table, ints, mine)
    return out.reshape(tile_rows, local_j, num_virt)


def shards(half_ints, coeffs, pair_map, tile_table):
    num_i, sblock, local_j, num_basis = half_ints.shape
    num_virt = coeffs.shape[1]
    num_pair = lax.axis_size("pair")
    fits = (
        num_i == 2 and local_j == 1 and lax.axis_size("occ") == 4 and num_pair == 8
        and sblock % 16 == 0 and sblock * num_pair == num_basis and num_basis == 7 * LANES
        and coeffs.shape[0] * 4 == num_basis and coeffs.shape[0] % 16 == 0
        and num_virt % (6 * LANES) == 0 and num_virt % (16 * (num_pair // num_i)) == 0
    )
    body = shards_kernel if fits else shards_general
    return body(half_ints, coeffs, pair_map, tile_table)


def solution(mesh):
    placed = (P(None, "pair", "occ", None), P("occ", None), P(), P())
    return jax.shard_map(
        shards, mesh=mesh, in_specs=placed, out_specs=P("pair", "occ", None), check_vma=False
    )
```

```python
import functools

import jax
import jax.numpy as jnp
from jax import lax
from jax.experimental import pallas as pl
from jax.experimental.pallas import tpu as pltpu
from jax.sharding import PartitionSpec as P


def shards_general(half_ints, coeffs, pair_map, tile_table):
    num_occ = half_ints.shape[0]
    sblock = half_ints.shape[1]
    local_j = half_ints.shape[2]
    num_basis = half_ints.shape[3]
    num_virt = coeffs.shape[1]
    num_pair = lax.axis_size("pair")
    tile_rows = num_occ * num_virt // num_pair
    all_coeffs = lax.all_gather(coeffs, "occ", axis=0, tiled=True)
    flat_ints = half_ints.reshape(num_occ * sblock * local_j, num_basis)
    half_mo = jnp.dot(flat_ints, all_coeffs, preferred_element_type=jnp.float32).astype(
        jnp.bfloat16
    )
    tile_id = jnp.sum(
        jnp.where(jnp.arange(num_pair) == lax.axis_index("pair"), tile_table, 0)
    )
    virt_start = tile_id * tile_rows % num_virt
    column_coeffs = lax.dynamic_slice_in_dim(all_coeffs, virt_start, tile_rows, 1)
    half_flat = half_mo.reshape(num_occ, sblock, local_j * num_virt)
    slot_occ = (tile_table * tile_rows // num_virt)[:, None, None]
    outgoing = jnp.broadcast_to(half_flat[:1], (num_pair,) + half_flat.shape[1:])
    for i in range(1, num_occ):
        outgoing = jnp.where(slot_occ == i, half_flat[i:i + 1], outgoing)
    incoming = lax.all_to_all(outgoing, "pair", split_axis=0, concat_axis=0, tiled=True)
    chosen = (pair_map[:, None] == jnp.arange(num_pair)[None, :]).astype(jnp.bfloat16)
    block_coeffs = jnp.einsum(
        "pg,gsa->psa", chosen, column_coeffs.reshape(num_pair, sblock, tile_rows),
        preferred_element_type=jnp.float32,
    ).astype(jnp.bfloat16)
    result = jnp.einsum("psa,psc->ac", block_coeffs, incoming, preferred_element_type=jnp.float32)
    return result.reshape(tile_rows, local_j, num_virt)


LANES = 128
ORDER_A = (0, 6, 1, 7, 2, 3, 4, 5)
ORDER_B = (0, 6, 1, 7, 2, 3, 4, 5)


def kernel(
    num_pair, num_i, local_tiles,
    pm_hbm, tt_hbm, h_hbm, c_hbm, o_ref,
    pm_ref, tt_ref, c_all, ct, hs, hr, ts, tr, out_sum,
    h_sem, c_sem, s_sem, x_send, x_recv, y_send, y_recv, f_send, f_recv, p_send, p_recv,
    h_send, h_recv, t_send, t_recv, ready,
):
    me = lax.axis_index("pair")
    occ = lax.axis_index("occ")
    z, y = me // 2, lax.rem(me, 2)
    core = lax.rem(occ, 2)
    num_basis, num_virt = c_all.shape
    crows = c_hbm.shape[0]
    sblock = h_hbm.shape[1]
    tile_rows = num_virt // local_tiles
    per_row = num_virt // LANES
    num_cols = num_basis // LANES
    middle = num_cols // 2
    partner = occ + 1 - 2 * core
    cross = lax.rem(occ + 2, 4)
    MESH = pl.DeviceIdType.MESH

    def column(plane, line):
        place = 2 * (lax.rem(plane + 1, 4) // 2) + lax.rem(line + core, 2)
        return middle + (2 * (plane // 2) - 1) * place

    mine = column(z, y)
    shared = mine == middle
    far_planes = (lax.rem(z + 2, 4), 3 - z)
    near_plane = z + 1 - 2 * lax.rem(z, 2)
    line_a = (lax.rem(z + 1, 4) // 2) * (1 - core) + (1 - (lax.rem(z + 1, 4) // 2)) * (1 - y)
    far = [(plane, line) for line in (line_a, 1 - line_a) for plane in far_planes]
    near = [(near_plane, line_a), (z, 1 - y), (near_plane, 1 - line_a)]
    peers = [(2 * plane + line, column(plane, line)) for plane, line in far + near]

    def remote(source, target, send, recv, where):
        return pltpu.make_async_remote_copy(
            src_ref=source, dst_ref=target, send_sem=send, recv_sem=recv,
            device_id=where, device_id_type=MESH,
        )

    barrier = pltpu.get_barrier_semaphore()
    inner = lax.rem(z + 1, 4) // 2 == 1
    outer = lax.rem(z + 1, 4) // 2 == 0
    alike = [1, 3, 5]
    unlike = [0, 2, 4, 6]
    greeted = [{"occ": partner}, {"occ": cross}] + [{"pair": peers[n][0]} for n in alike]

    def greet(semaphore, where):
        pl.semaphore_signal(semaphore, inc=1, device_id=where, device_id_type=MESH)

    for peer in greeted:
        greet(barrier, peer)

    @pl.when(inner)
    def _():
        for n in unlike:
            greet(barrier, {"pair": peers[n][0]})

    mine_rows = pl.ds(pl.multiple_of(crows * occ, crows), crows)
    cross_rows = pl.ds(pl.multiple_of(crows * cross, crows), crows)

    def cols(m):
        return pl.ds(pl.multiple_of(m * LANES, LANES), LANES)

    lent = 1
    back = per_row - lent
    given = [back * y + k for k in range(lent)]
    plain = list(range(lent, back))
    taken = [back * (1 - y) + k for k in range(lent)]
    fetched = given + plain
    arriving = fetched + taken

    def h_column(m):
        return h_hbm.at[:, :, cols(m)]

    fetch_c = [
        pltpu.make_async_copy(c_hbm.at[:, cols(m)], c_all.at[mine_rows, cols(m)], c_sem.at[k])
        for k, m in enumerate(arriving)]
    fetch_h = [
        pltpu.make_async_copy(h_column(m), hs.at[n], h_sem.at[n]) for n, (_, m) in enumerate(peers)]
    fetch_own = pltpu.make_async_copy(h_column(mine), hr.at[me], h_sem.at[len(peers)])
    fetch_pm = pltpu.make_async_copy(pm_hbm, pm_ref, s_sem.at[0])
    fetch_tt = pltpu.make_async_copy(tt_hbm, tt_ref, s_sem.at[1])
    for fetch in fetch_h + fetch_c + [fetch_own, fetch_pm, fetch_tt]:
        fetch.start()

    def passed(m, send, recv, where):
        spot = c_all.at[cross_rows, cols(m)]
        return remote(spot, spot, send, recv, where)

    to_cross = []
    for k, m in enumerate(fetched):
        spot = c_all.at[mine_rows, cols(m)]
        to_cross.append(remote(spot, spot, x_send.at[k], x_recv.at[k], {"occ": cross}))
    relay = [passed(m, f_send.at[k], f_recv.at[k], {"occ": partner}) for k, m in enumerate(arriving)]
    lend = [passed(m, y_send.at[k], y_recv.at[k], {"pair": 2 * z + 1 - y}) for k, m in enumerate(given)]
    borrow = [passed(m, y_send.at[k], y_recv.at[k], {"pair": 2 * z + 1 - y}) for k, m in enumerate(taken)]
    block = c_all.at[mine_rows, :]
    to_partner = remote(block, block, p_send, p_recv, {"occ": partner})
    h_copies = [
        remote(hs.at[n], hr.at[me], h_send.at[n], h_recv.at[me], {"pair": p}) for n, (p, _) in enumerate(peers)]
    h_arrivals = [
        remote(hs.at[n], hr.at[p], h_send.at[n], h_recv.at[p], {"pair": p}) for n, (p, _) in enumerate(peers)]

    served = [a + (b - a) * (z // 2) for a, b in zip(ORDER_A, ORDER_B)]

    def t_copy(p):
        return remote(ts.at[p], tr.at[mine], t_send.at[p], t_recv.at[mine], {"pair": p})

    def t_arrival(m):
        return remote(ts.at[0], tr.at[m], t_send.at[0], t_recv.at[m], {"pair": me})

    for fetch in fetch_c + fetch_h:
        fetch.wait()

    @pl.when(inner)
    def _():
        pl.semaphore_wait(barrier, len(greeted))

    @pl.when(outer)
    def _():
        pl.semaphore_wait(barrier, len(greeted) + len(unlike))
        for n in unlike:
            greet(ready, {"pair": peers[n][0]})

    for copy in to_cross[:lent]:
        copy.start()

    @pl.when(outer)
    def _():
        for copy in h_copies[:2]:
            copy.start()

    @pl.when(inner)
    def _():
        for n in alike:
            h_copies[n].start()

    for copy in to_cross[lent:]:
        copy.start()
    to_partner.start()

    @pl.when(outer)
    def _():
        for copy in h_copies[2:]:
            copy.start()

    @pl.when(inner)
    def _():
        pl.semaphore_wait(ready, len(unlike))
        for n in (0, 4, 2, 6):
            h_copies[n].start()


    def turn(m):
        row = m * LANES
        while row < (m + 1) * LANES:
            j, start = row // tile_rows, row % tile_rows
            count = min(tile_rows - start, (m + 1) * LANES - row)
            ct[j, start:start + count, :] = c_all[:, m * LANES:(m + 1) * LANES].T[row - m * LANES:row - m * LANES + count]
            row += count

    for fetch in (fetch_own, fetch_pm, fetch_tt):
        fetch.wait()
    slot = []
    for g in range(num_pair):
        found = 0
        for p in range(1, num_pair):
            found = jnp.where(pm_ref[p] == g, p, found)
        slot.append(found)
    to_partner.wait_recv()

    def turn_edge(here):
        @pl.when(here == 0)
        def _():
            for m in range(lent):
                turn(m)

        @pl.when(here == 1)
        def _():
            for m in range(back, per_row):
                turn(m)

    for k in range(lent):
        to_cross[k].wait_recv()
        lend[k].start()
        relay[k].start()
    for k in range(lent):
        relay[k].wait_recv()
    turn_edge(y)
    for k in range(max(len(plain), lent)):
        if k < len(plain):
            to_cross[lent + k].wait_recv()
            relay[lent + k].start()
        if k < lent:
            borrow[k].wait_recv()
            relay[back + k].start()
    for k in range(len(plain)):
        relay[lent + k].wait_recv()
        turn(lent + k)
    for k in range(lent):
        relay[back + k].wait_recv()
    turn_edge(1 - y)
    for copy in h_arrivals:
        copy.wait_recv()

    def tile(p):
        t = tt_ref[p]
        i = jnp.where(t >= local_tiles, 1, 0)
        block = jnp.concatenate([hr[slot[g], i] for g in range(num_pair)], axis=0)
        return jnp.dot(ct[t - local_tiles * i], block, preferred_element_type=jnp.float32).astype(jnp.bfloat16)

    def sends(p):
        away = z // 2 != p // (num_pair // 2)
        return jnp.logical_and(me != p, jnp.logical_not(jnp.logical_and(shared, away)))

    for p in served:
        @pl.when(sends(p))
        def _():
            ts[p] = tile(p)
            t_copy(p).start()
    tr[mine] = tile(me)

    own_base = (z // 2) * middle
    far_base = (1 - z // 2) * (middle + 1)
    wide = 2 * LANES
    parts = ((own_base, middle + 1), (far_base, middle))
    for g, (base, count) in enumerate(parts):
        for u in range(count):
            if g == 0:
                pl.when(base + u != mine)(t_arrival(base + u).wait_recv)
            else:
                t_arrival(base + u).wait_recv()
        block = jnp.concatenate([tr[base + u] for u in range(count)], axis=1)
        rows = pl.ds(pl.multiple_of(base * LANES, LANES), count * LANES)
        for n in range(num_virt // wide):
            span = slice(n * wide, (n + 1) * wide)
            total = jnp.dot(block, c_all[rows, span], preferred_element_type=jnp.float32)
            if g > 0:
                total = total + out_sum[:, span]
            if g < len(parts) - 1:
                out_sum[:, span] = total
            else:
                for m in range(2):
                    o_ref[pl.ds(2 * n + m, tile_rows, stride=per_row), :] = total[:, m * LANES:(m + 1) * LANES]

    for copy in to_cross + lend + relay + [to_partner] + h_copies:
        copy.wait_send()
    for p in served:
        pl.when(sends(p))(t_copy(p).wait_send)


def shards_kernel(half_ints, coeffs, pair_map, tile_table):
    num_i, sblock, local_j, num_basis = half_ints.shape
    num_virt = coeffs.shape[1]
    num_pair = lax.axis_size("pair")
    local_tiles = num_pair // num_i
    tile_rows = num_virt // local_tiles
    per_row = num_virt // LANES
    num_cols = num_basis // LANES
    ints = half_ints.reshape(num_i, sblock, num_basis)
    bf16 = jnp.bfloat16
    dma = pltpu.SemaphoreType.DMA
    vmem = pl.BlockSpec(memory_space=pltpu.VMEM)
    hbm = pl.BlockSpec(memory_space=pltpu.HBM)
    ints, mine, pair_map, tile_table = (
        pltpu.with_memory_space_constraint(a, pltpu.HBM) for a in (ints, coeffs, pair_map, tile_table))
    out = pl.pallas_call(
        functools.partial(kernel, num_pair, num_i, local_tiles),
        out_shape=jax.ShapeDtypeStruct((tile_rows * per_row, LANES), jnp.float32),
        in_specs=[hbm, hbm, hbm, hbm],
        out_specs=vmem,
        scratch_shapes=[
            pltpu.SMEM(pair_map.shape, jnp.int32),
            pltpu.SMEM(tile_table.shape, jnp.int32),
            pltpu.VMEM((num_basis, num_virt), bf16),
            pltpu.VMEM((local_tiles, tile_rows, num_basis), bf16),
            pltpu.VMEM((num_pair - 1, num_i, sblock, LANES), bf16),
            pltpu.VMEM((num_pair, num_i, sblock, LANES), bf16),
            pltpu.VMEM((num_pair, tile_rows, LANES), bf16),
            pltpu.VMEM((num_cols, tile_rows, LANES), bf16),
            pltpu.VMEM((tile_rows, num_virt), jnp.float32),
            dma((num_pair,)), dma((per_row,)), dma((2,)),
            dma((per_row,)), dma((per_row,)), dma((per_row,)), dma((per_row,)), dma((per_row,)), dma((per_row,)),
            dma, dma,
            dma((num_pair - 1,)), dma((num_pair,)), dma((num_pair,)), dma((num_cols,)),
            pltpu.SemaphoreType.REGULAR,
        ],
        compiler_params=pltpu.CompilerParams(
            collective_id=0, has_side_effects=True, vmem_limit_bytes=40 * 1024 * 1024),
    )(pair_map, tile_table, ints, mine)
    return out.reshape(tile_rows, local_j, num_virt)


def shards(half_ints, coeffs, pair_map, tile_table):
    num_i, sblock, local_j, num_basis = half_ints.shape
    num_virt = coeffs.shape[1]
    num_pair = lax.axis_size("pair")
    fits = (
        num_i == 2 and local_j == 1 and lax.axis_size("occ") == 4 and num_pair == 8
        and sblock % 16 == 0 and sblock * num_pair == num_basis and num_basis == 7 * LANES
        and coeffs.shape[0] * 4 == num_basis and coeffs.shape[0] % 16 == 0
        and num_virt % (6 * LANES) == 0 and num_virt % (16 * (num_pair // num_i)) == 0
    )
    body = shards_kernel if fits else shards_general
    return body(half_ints, coeffs, pair_map, tile_table)


def solution(mesh):
    placed = (P(None, "pair", "occ", None), P("occ", None), P(), P())
    return jax.shard_map(
        shards, mesh=mesh, in_specs=placed, out_specs=P("pair", "occ", None), check_vma=False
    )
```

```python
import functools

import jax
import jax.numpy as jnp
from jax import lax
from jax.experimental import pallas as pl
from jax.experimental.pallas import tpu as pltpu
from jax.sharding import PartitionSpec as P


def shards_general(half_ints, coeffs, pair_map, tile_table):
    num_occ = half_ints.shape[0]
    sblock = half_ints.shape[1]
    local_j = half_ints.shape[2]
    num_basis = half_ints.shape[3]
    num_virt = coeffs.shape[1]
    num_pair = lax.axis_size("pair")
    tile_rows = num_occ * num_virt // num_pair
    all_coeffs = lax.all_gather(coeffs, "occ", axis=0, tiled=True)
    flat_ints = half_ints.reshape(num_occ * sblock * local_j, num_basis)
    half_mo = jnp.dot(flat_ints, all_coeffs, preferred_element_type=jnp.float32).astype(
        jnp.bfloat16
    )
    tile_id = jnp.sum(
        jnp.where(jnp.arange(num_pair) == lax.axis_index("pair"), tile_table, 0)
    )
    virt_start = tile_id * tile_rows % num_virt
    column_coeffs = lax.dynamic_slice_in_dim(all_coeffs, virt_start, tile_rows, 1)
    half_flat = half_mo.reshape(num_occ, sblock, local_j * num_virt)
    slot_occ = (tile_table * tile_rows // num_virt)[:, None, None]
    outgoing = jnp.broadcast_to(half_flat[:1], (num_pair,) + half_flat.shape[1:])
    for i in range(1, num_occ):
        outgoing = jnp.where(slot_occ == i, half_flat[i:i + 1], outgoing)
    incoming = lax.all_to_all(outgoing, "pair", split_axis=0, concat_axis=0, tiled=True)
    chosen = (pair_map[:, None] == jnp.arange(num_pair)[None, :]).astype(jnp.bfloat16)
    block_coeffs = jnp.einsum(
        "pg,gsa->psa", chosen, column_coeffs.reshape(num_pair, sblock, tile_rows),
        preferred_element_type=jnp.float32,
    ).astype(jnp.bfloat16)
    result = jnp.einsum("psa,psc->ac", block_coeffs, incoming, preferred_element_type=jnp.float32)
    return result.reshape(tile_rows, local_j, num_virt)


LANES = 128
ORDER_A = (0, 4, 1, 5, 2, 3, 6, 7)
ORDER_B = (0, 4, 1, 5, 2, 3, 6, 7)


def kernel(
    num_pair, num_i, local_tiles,
    pm_hbm, tt_hbm, h_hbm, c_hbm, o_ref,
    pm_ref, tt_ref, c_all, ct, hs, hr, ts, tr, out_sum,
    h_sem, c_sem, s_sem, x_send, x_recv, y_send, y_recv, f_send, f_recv, p_send, p_recv,
    h_send, h_recv, t_send, t_recv, ready,
):
    me = lax.axis_index("pair")
    occ = lax.axis_index("occ")
    z, y = me // 2, lax.rem(me, 2)
    core = lax.rem(occ, 2)
    num_basis, num_virt = c_all.shape
    crows = c_hbm.shape[0]
    sblock = h_hbm.shape[1]
    tile_rows = num_virt // local_tiles
    per_row = num_virt // LANES
    num_cols = num_basis // LANES
    middle = num_cols // 2
    partner = occ + 1 - 2 * core
    cross = lax.rem(occ + 2, 4)
    MESH = pl.DeviceIdType.MESH

    def column(plane, line):
        place = 2 * (lax.rem(plane + 1, 4) // 2) + lax.rem(line + core, 2)
        return middle + (2 * (plane // 2) - 1) * place

    mine = column(z, y)
    shared = mine == middle
    far_planes = (lax.rem(z + 2, 4), 3 - z)
    near_plane = z + 1 - 2 * lax.rem(z, 2)
    line_a = (lax.rem(z + 1, 4) // 2) * (1 - core) + (1 - (lax.rem(z + 1, 4) // 2)) * (1 - y)
    far = [(plane, line) for line in (line_a, 1 - line_a) for plane in far_planes]
    near = [(near_plane, line_a), (z, 1 - y), (near_plane, 1 - line_a)]
    peers = [(2 * plane + line, column(plane, line)) for plane, line in far + near]

    def remote(source, target, send, recv, where):
        return pltpu.make_async_remote_copy(
            src_ref=source, dst_ref=target, send_sem=send, recv_sem=recv,
            device_id=where, device_id_type=MESH,
        )

    barrier = pltpu.get_barrier_semaphore()
    inner = lax.rem(z + 1, 4) // 2 == 1
    outer = lax.rem(z + 1, 4) // 2 == 0
    alike = [1, 3, 5]
    unlike = [0, 2, 4, 6]
    greeted = [{"occ": partner}, {"occ": cross}] + [{"pair": peers[n][0]} for n in alike]

    def greet(semaphore, where):
        pl.semaphore_signal(semaphore, inc=1, device_id=where, device_id_type=MESH)

    for peer in greeted:
        greet(barrier, peer)

    @pl.when(inner)
    def _():
        for n in unlike:
            greet(barrier, {"pair": peers[n][0]})

    mine_rows = pl.ds(pl.multiple_of(crows * occ, crows), crows)
    cross_rows = pl.ds(pl.multiple_of(crows * cross, crows), crows)

    def cols(m):
        return pl.ds(pl.multiple_of(m * LANES, LANES), LANES)

    lent = 1
    back = per_row - lent
    given = [back * y + k for k in range(lent)]
    plain = list(range(lent, back))
    taken = [back * (1 - y) + k for k in range(lent)]
    fetched = given + plain
    arriving = fetched + taken

    def h_column(m):
        return h_hbm.at[:, :, cols(m)]

    fetch_c = [
        pltpu.make_async_copy(c_hbm.at[:, cols(m)], c_all.at[mine_rows, cols(m)], c_sem.at[k])
        for k, m in enumerate(arriving)]
    fetch_h = [
        pltpu.make_async_copy(h_column(m), hs.at[n], h_sem.at[n]) for n, (_, m) in enumerate(peers)]
    fetch_own = pltpu.make_async_copy(h_column(mine), hr.at[me], h_sem.at[len(peers)])
    fetch_pm = pltpu.make_async_copy(pm_hbm, pm_ref, s_sem.at[0])
    fetch_tt = pltpu.make_async_copy(tt_hbm, tt_ref, s_sem.at[1])
    for fetch in fetch_h + fetch_c + [fetch_own, fetch_pm, fetch_tt]:
        fetch.start()

    def passed(m, send, recv, where):
        spot = c_all.at[cross_rows, cols(m)]
        return remote(spot, spot, send, recv, where)

    to_cross = []
    for k, m in enumerate(fetched):
        spot = c_all.at[mine_rows, cols(m)]
        to_cross.append(remote(spot, spot, x_send.at[k], x_recv.at[k], {"occ": cross}))
    relay = [passed(m, f_send.at[k], f_recv.at[k], {"occ": partner}) for k, m in enumerate(arriving)]
    lend = [passed(m, y_send.at[k], y_recv.at[k], {"pair": 2 * z + 1 - y}) for k, m in enumerate(given)]
    borrow = [passed(m, y_send.at[k], y_recv.at[k], {"pair": 2 * z + 1 - y}) for k, m in enumerate(taken)]
    block = c_all.at[mine_rows, :]
    to_partner = remote(block, block, p_send, p_recv, {"occ": partner})
    h_copies = [
        remote(hs.at[n], hr.at[me], h_send.at[n], h_recv.at[me], {"pair": p}) for n, (p, _) in enumerate(peers)]
    h_arrivals = [
        remote(hs.at[n], hr.at[p], h_send.at[n], h_recv.at[p], {"pair": p}) for n, (p, _) in enumerate(peers)]

    served = [a + (b - a) * (z // 2) for a, b in zip(ORDER_A, ORDER_B)]

    def t_copy(p):
        return remote(ts.at[p], tr.at[mine], t_send.at[p], t_recv.at[mine], {"pair": p})

    def t_arrival(m):
        return remote(ts.at[0], tr.at[m], t_send.at[0], t_recv.at[m], {"pair": me})

    for fetch in fetch_c + fetch_h:
        fetch.wait()

    @pl.when(inner)
    def _():
        pl.semaphore_wait(barrier, len(greeted))

    @pl.when(outer)
    def _():
        pl.semaphore_wait(barrier, len(greeted) + len(unlike))
        for n in unlike:
            greet(ready, {"pair": peers[n][0]})

    for copy in to_cross[:lent]:
        copy.start()

    @pl.when(outer)
    def _():
        for copy in h_copies[:2]:
            copy.start()

    @pl.when(inner)
    def _():
        for n in alike:
            h_copies[n].start()

    for copy in to_cross[lent:]:
        copy.start()
    to_partner.start()

    @pl.when(outer)
    def _():
        for copy in h_copies[2:]:
            copy.start()

    @pl.when(inner)
    def _():
        pl.semaphore_wait(ready, len(unlike))
        for n in (0, 4, 2, 6):
            h_copies[n].start()


    def turn(m):
        row = m * LANES
        while row < (m + 1) * LANES:
            j, start = row // tile_rows, row % tile_rows
            count = min(tile_rows - start, (m + 1) * LANES - row)
            ct[j, start:start + count, :] = c_all[:, m * LANES:(m + 1) * LANES].T[row - m * LANES:row - m * LANES + count]
            row += count

    for fetch in (fetch_own, fetch_pm, fetch_tt):
        fetch.wait()
    slot = []
    for g in range(num_pair):
        found = 0
        for p in range(1, num_pair):
            found = jnp.where(pm_ref[p] == g, p, found)
        slot.append(found)
    to_partner.wait_recv()

    def turn_edge(here):
        @pl.when(here == 0)
        def _():
            for m in range(lent):
                turn(m)

        @pl.when(here == 1)
        def _():
            for m in range(back, per_row):
                turn(m)

    for k in range(lent):
        to_cross[k].wait_recv()
        lend[k].start()
        relay[k].start()
    for k in range(lent):
        relay[k].wait_recv()
    turn_edge(y)
    for k in range(len(plain)):
        to_cross[lent + k].wait_recv()
        relay[lent + k].start()
    for k in range(lent):
        borrow[k].wait_recv()
        relay[back + k].start()
    for k in range(len(plain)):
        relay[lent + k].wait_recv()
        turn(lent + k)
    for k in range(lent):
        relay[back + k].wait_recv()
    turn_edge(1 - y)
    for copy in h_arrivals:
        copy.wait_recv()

    def tile(p):
        t = tt_ref[p]
        i = jnp.where(t >= local_tiles, 1, 0)
        block = jnp.concatenate([hr[slot[g], i] for g in range(num_pair)], axis=0)
        return jnp.dot(ct[t - local_tiles * i], block, preferred_element_type=jnp.float32).astype(jnp.bfloat16)

    def sends(p):
        away = z // 2 != p // (num_pair // 2)
        return jnp.logical_and(me != p, jnp.logical_not(jnp.logical_and(shared, away)))

    for p in served:
        @pl.when(sends(p))
        def _():
            ts[p] = tile(p)
            t_copy(p).start()
    tr[mine] = tile(me)

    own_base = (z // 2) * middle
    far_base = (1 - z // 2) * (middle + 1)
    wide = 2 * LANES
    parts = ((own_base, middle + 1), (far_base, middle))
    for g, (base, count) in enumerate(parts):
        for u in range(count):
            if g == 0:
                pl.when(base + u != mine)(t_arrival(base + u).wait_recv)
            else:
                t_arrival(base + u).wait_recv()
        block = jnp.concatenate([tr[base + u] for u in range(count)], axis=1)
        rows = pl.ds(pl.multiple_of(base * LANES, LANES), count * LANES)
        for n in range(num_virt // wide):
            span = slice(n * wide, (n + 1) * wide)
            total = jnp.dot(block, c_all[rows, span], preferred_element_type=jnp.float32)
            if g > 0:
                total = total + out_sum[:, span]
            if g < len(parts) - 1:
                out_sum[:, span] = total
            else:
                for m in range(2):
                    o_ref[pl.ds(2 * n + m, tile_rows, stride=per_row), :] = total[:, m * LANES:(m + 1) * LANES]

    for copy in to_cross + lend + relay + [to_partner] + h_copies:
        copy.wait_send()
    for p in served:
        pl.when(sends(p))(t_copy(p).wait_send)


def shards_kernel(half_ints, coeffs, pair_map, tile_table):
    num_i, sblock, local_j, num_basis = half_ints.shape
    num_virt = coeffs.shape[1]
    num_pair = lax.axis_size("pair")
    local_tiles = num_pair // num_i
    tile_rows = num_virt // local_tiles
    per_row = num_virt // LANES
    num_cols = num_basis // LANES
    ints = half_ints.reshape(num_i, sblock, num_basis)
    bf16 = jnp.bfloat16
    dma = pltpu.SemaphoreType.DMA
    vmem = pl.BlockSpec(memory_space=pltpu.VMEM)
    hbm = pl.BlockSpec(memory_space=pltpu.HBM)
    ints, mine, pair_map, tile_table = (
        pltpu.with_memory_space_constraint(a, pltpu.HBM) for a in (ints, coeffs, pair_map, tile_table))
    out = pl.pallas_call(
        functools.partial(kernel, num_pair, num_i, local_tiles),
        out_shape=jax.ShapeDtypeStruct((tile_rows * per_row, LANES), jnp.float32),
        in_specs=[hbm, hbm, hbm, hbm],
        out_specs=vmem,
        scratch_shapes=[
            pltpu.SMEM(pair_map.shape, jnp.int32),
            pltpu.SMEM(tile_table.shape, jnp.int32),
            pltpu.VMEM((num_basis, num_virt), bf16),
            pltpu.VMEM((local_tiles, tile_rows, num_basis), bf16),
            pltpu.VMEM((num_pair - 1, num_i, sblock, LANES), bf16),
            pltpu.VMEM((num_pair, num_i, sblock, LANES), bf16),
            pltpu.VMEM((num_pair, tile_rows, LANES), bf16),
            pltpu.VMEM((num_cols, tile_rows, LANES), bf16),
            pltpu.VMEM((tile_rows, num_virt), jnp.float32),
            dma((num_pair,)), dma((per_row,)), dma((2,)),
            dma((per_row,)), dma((per_row,)), dma((per_row,)), dma((per_row,)), dma((per_row,)), dma((per_row,)),
            dma, dma,
            dma((num_pair - 1,)), dma((num_pair,)), dma((num_pair,)), dma((num_cols,)),
            pltpu.SemaphoreType.REGULAR,
        ],
        compiler_params=pltpu.CompilerParams(
            collective_id=0, has_side_effects=True, vmem_limit_bytes=40 * 1024 * 1024),
    )(pair_map, tile_table, ints, mine)
    return out.reshape(tile_rows, local_j, num_virt)


def shards(half_ints, coeffs, pair_map, tile_table):
    num_i, sblock, local_j, num_basis = half_ints.shape
    num_virt = coeffs.shape[1]
    num_pair = lax.axis_size("pair")
    fits = (
        num_i == 2 and local_j == 1 and lax.axis_size("occ") == 4 and num_pair == 8
        and sblock % 16 == 0 and sblock * num_pair == num_basis and num_basis == 7 * LANES
        and coeffs.shape[0] * 4 == num_basis and coeffs.shape[0] % 16 == 0
        and num_virt % (6 * LANES) == 0 and num_virt % (16 * (num_pair // num_i)) == 0
    )
    body = shards_kernel if fits else shards_general
    return body(half_ints, coeffs, pair_map, tile_table)


def solution(mesh):
    placed = (P(None, "pair", "occ", None), P("occ", None), P(), P())
    return jax.shard_map(
        shards, mesh=mesh, in_specs=placed, out_specs=P("pair", "occ", None), check_vma=False
    )
```

```python
import functools

import jax
import jax.numpy as jnp
from jax import lax
from jax.experimental import pallas as pl
from jax.experimental.pallas import tpu as pltpu
from jax.sharding import PartitionSpec as P


def shards_general(half_ints, coeffs, pair_map, tile_table):
    num_occ = half_ints.shape[0]
    sblock = half_ints.shape[1]
    local_j = half_ints.shape[2]
    num_basis = half_ints.shape[3]
    num_virt = coeffs.shape[1]
    num_pair = lax.axis_size("pair")
    tile_rows = num_occ * num_virt // num_pair
    all_coeffs = lax.all_gather(coeffs, "occ", axis=0, tiled=True)
    flat_ints = half_ints.reshape(num_occ * sblock * local_j, num_basis)
    half_mo = jnp.dot(flat_ints, all_coeffs, preferred_element_type=jnp.float32).astype(
        jnp.bfloat16
    )
    tile_id = jnp.sum(
        jnp.where(jnp.arange(num_pair) == lax.axis_index("pair"), tile_table, 0)
    )
    virt_start = tile_id * tile_rows % num_virt
    column_coeffs = lax.dynamic_slice_in_dim(all_coeffs, virt_start, tile_rows, 1)
    half_flat = half_mo.reshape(num_occ, sblock, local_j * num_virt)
    slot_occ = (tile_table * tile_rows // num_virt)[:, None, None]
    outgoing = jnp.broadcast_to(half_flat[:1], (num_pair,) + half_flat.shape[1:])
    for i in range(1, num_occ):
        outgoing = jnp.where(slot_occ == i, half_flat[i:i + 1], outgoing)
    incoming = lax.all_to_all(outgoing, "pair", split_axis=0, concat_axis=0, tiled=True)
    chosen = (pair_map[:, None] == jnp.arange(num_pair)[None, :]).astype(jnp.bfloat16)
    block_coeffs = jnp.einsum(
        "pg,gsa->psa", chosen, column_coeffs.reshape(num_pair, sblock, tile_rows),
        preferred_element_type=jnp.float32,
    ).astype(jnp.bfloat16)
    result = jnp.einsum("psa,psc->ac", block_coeffs, incoming, preferred_element_type=jnp.float32)
    return result.reshape(tile_rows, local_j, num_virt)


LANES = 128
ORDER_A = (0, 6, 1, 7, 2, 3, 4, 5)
ORDER_B = (0, 6, 1, 7, 2, 3, 4, 5)


def kernel(
    num_pair, num_i, local_tiles,
    pm_hbm, tt_hbm, h_hbm, c_hbm, o_ref,
    pm_ref, tt_ref, c_all, ct, hs, hr, ts, tr, out_sum,
    h_sem, c_sem, s_sem, x_send, x_recv, y_send, y_recv, f_send, f_recv, p_send, p_recv,
    h_send, h_recv, t_send, t_recv, ready,
):
    me = lax.axis_index("pair")
    occ = lax.axis_index("occ")
    z, y = me // 2, lax.rem(me, 2)
    core = lax.rem(occ, 2)
    num_basis, num_virt = c_all.shape
    crows = c_hbm.shape[0]
    sblock = h_hbm.shape[1]
    tile_rows = num_virt // local_tiles
    per_row = num_virt // LANES
    num_cols = num_basis // LANES
    middle = num_cols // 2
    partner = occ + 1 - 2 * core
    cross = lax.rem(occ + 2, 4)
    MESH = pl.DeviceIdType.MESH

    def column(plane, line):
        place = 2 * (lax.rem(plane + 1, 4) // 2) + lax.rem(line + core, 2)
        return middle + (2 * (plane // 2) - 1) * place

    mine = column(z, y)
    shared = mine == middle
    far_planes = (lax.rem(z + 2, 4), 3 - z)
    near_plane = z + 1 - 2 * lax.rem(z, 2)
    line_a = (lax.rem(z + 1, 4) // 2) * (1 - core) + (1 - (lax.rem(z + 1, 4) // 2)) * (1 - y)
    far = [(plane, line) for line in (line_a, 1 - line_a) for plane in far_planes]
    near = [(near_plane, line_a), (z, 1 - y), (near_plane, 1 - line_a)]
    peers = [(2 * plane + line, column(plane, line)) for plane, line in far + near]

    def remote(source, target, send, recv, where):
        return pltpu.make_async_remote_copy(
            src_ref=source, dst_ref=target, send_sem=send, recv_sem=recv,
            device_id=where, device_id_type=MESH,
        )

    barrier = pltpu.get_barrier_semaphore()
    inner = lax.rem(z + 1, 4) // 2 == 1
    outer = lax.rem(z + 1, 4) // 2 == 0
    alike = [1, 3, 5]
    unlike = [0, 2, 4, 6]
    greeted = [{"occ": partner}, {"occ": cross}] + [{"pair": peers[n][0]} for n in alike]

    def greet(semaphore, where):
        pl.semaphore_signal(semaphore, inc=1, device_id=where, device_id_type=MESH)

    for peer in greeted:
        greet(barrier, peer)

    @pl.when(inner)
    def _():
        for n in unlike:
            greet(barrier, {"pair": peers[n][0]})

    mine_rows = pl.ds(pl.multiple_of(crows * occ, crows), crows)
    cross_rows = pl.ds(pl.multiple_of(crows * cross, crows), crows)

    def cols(m):
        return pl.ds(pl.multiple_of(m * LANES, LANES), LANES)

    lent = 1
    back = per_row - lent
    given = [back * y + k for k in range(lent)]
    plain = list(range(lent, back))
    taken = [back * (1 - y) + k for k in range(lent)]
    fetched = given + plain
    arriving = fetched + taken

    def h_column(m):
        return h_hbm.at[:, :, cols(m)]

    fetch_c = [
        pltpu.make_async_copy(c_hbm.at[:, cols(m)], c_all.at[mine_rows, cols(m)], c_sem.at[k])
        for k, m in enumerate(arriving)]
    fetch_h = [
        pltpu.make_async_copy(h_column(m), hs.at[n], h_sem.at[n]) for n, (_, m) in enumerate(peers)]
    fetch_own = pltpu.make_async_copy(h_column(mine), hr.at[me], h_sem.at[len(peers)])
    fetch_pm = pltpu.make_async_copy(pm_hbm, pm_ref, s_sem.at[0])
    fetch_tt = pltpu.make_async_copy(tt_hbm, tt_ref, s_sem.at[1])
    for fetch in fetch_c + fetch_h + [fetch_own, fetch_pm, fetch_tt]:
        fetch.start()

    def passed(m, send, recv, where):
        spot = c_all.at[cross_rows, cols(m)]
        return remote(spot, spot, send, recv, where)

    to_cross = []
    for k, m in enumerate(fetched):
        spot = c_all.at[mine_rows, cols(m)]
        to_cross.append(remote(spot, spot, x_send.at[k], x_recv.at[k], {"occ": cross}))
    relay = [passed(m, f_send.at[k], f_recv.at[k], {"occ": partner}) for k, m in enumerate(arriving)]
    lend = [passed(m, y_send.at[k], y_recv.at[k], {"pair": 2 * z + 1 - y}) for k, m in enumerate(given)]
    borrow = [passed(m, y_send.at[k], y_recv.at[k], {"pair": 2 * z + 1 - y}) for k, m in enumerate(taken)]
    block = c_all.at[mine_rows, :]
    to_partner = remote(block, block, p_send, p_recv, {"occ": partner})
    h_copies = [
        remote(hs.at[n], hr.at[me], h_send.at[n], h_recv.at[me], {"pair": p}) for n, (p, _) in enumerate(peers)]
    h_arrivals = [
        remote(hs.at[n], hr.at[p], h_send.at[n], h_recv.at[p], {"pair": p}) for n, (p, _) in enumerate(peers)]

    served = [a + (b - a) * (z // 2) for a, b in zip(ORDER_A, ORDER_B)]

    def t_copy(p):
        return remote(ts.at[p], tr.at[mine], t_send.at[p], t_recv.at[mine], {"pair": p})

    def t_arrival(m):
        return remote(ts.at[0], tr.at[m], t_send.at[0], t_recv.at[m], {"pair": me})

    def send_column(n):
        fetch_h[n].wait()
        h_copies[n].start()

    def send_tile(k):
        fetch_c[k].wait()
        to_cross[k].start()


    @pl.when(inner)
    def _():
        pl.semaphore_wait(barrier, len(greeted))

    @pl.when(outer)
    def _():
        pl.semaphore_wait(barrier, len(greeted) + len(unlike))
        for n in unlike:
            greet(ready, {"pair": peers[n][0]})

    for k in range(lent):
        send_tile(k)

    @pl.when(outer)
    def _():
        for n in range(2):
            send_column(n)

    @pl.when(inner)
    def _():
        for n in alike:
            send_column(n)

    for k in range(lent, len(fetched)):
        send_tile(k)
    for fetch in fetch_c[len(fetched):]:
        fetch.wait()
    to_partner.start()

    @pl.when(outer)
    def _():
        for n in range(2, len(peers)):
            send_column(n)

    @pl.when(inner)
    def _():
        pl.semaphore_wait(ready, len(unlike))
        for n in (0, 4, 2, 6):
            send_column(n)


    def turn(m):
        row = m * LANES
        while row < (m + 1) * LANES:
            j, start = row // tile_rows, row % tile_rows
            count = min(tile_rows - start, (m + 1) * LANES - row)
            ct[j, start:start + count, :] = c_all[:, m * LANES:(m + 1) * LANES].T[row - m * LANES:row - m * LANES + count]
            row += count

    for fetch in (fetch_own, fetch_pm, fetch_tt):
        fetch.wait()
    slot = []
    for g in range(num_pair):
        found = 0
        for p in range(1, num_pair):
            found = jnp.where(pm_ref[p] == g, p, found)
        slot.append(found)
    to_partner.wait_recv()

    def turn_edge(here):
        @pl.when(here == 0)
        def _():
            for m in range(lent):
                turn(m)

        @pl.when(here == 1)
        def _():
            for m in range(back, per_row):
                turn(m)

    for k in range(lent):
        to_cross[k].wait_recv()
        lend[k].start()
        relay[k].start()
    for k in range(lent):
        relay[k].wait_recv()
    turn_edge(y)
    for k in range(max(len(plain), lent)):
        if k < len(plain):
            to_cross[lent + k].wait_recv()
            relay[lent + k].start()
        if k < lent:
            borrow[k].wait_recv()
            relay[back + k].start()
    for k in range(len(plain)):
        relay[lent + k].wait_recv()
        turn(lent + k)
    for k in range(lent):
        relay[back + k].wait_recv()
    turn_edge(1 - y)
    for copy in h_arrivals:
        copy.wait_recv()

    def tile(p):
        t = tt_ref[p]
        i = jnp.where(t >= local_tiles, 1, 0)
        block = jnp.concatenate([hr[slot[g], i] for g in range(num_pair)], axis=0)
        return jnp.dot(ct[t - local_tiles * i], block, preferred_element_type=jnp.float32).astype(jnp.bfloat16)

    def sends(p):
        away = z // 2 != p // (num_pair // 2)
        return jnp.logical_and(me != p, jnp.logical_not(jnp.logical_and(shared, away)))

    for p in served:
        @pl.when(sends(p))
        def _():
            ts[p] = tile(p)
            t_copy(p).start()
    tr[mine] = tile(me)

    own_base = (z // 2) * middle
    far_base = (1 - z // 2) * (middle + 1)
    wide = 2 * LANES
    parts = ((own_base, middle + 1), (far_base, middle))
    for g, (base, count) in enumerate(parts):
        for u in range(count):
            if g == 0:
                pl.when(base + u != mine)(t_arrival(base + u).wait_recv)
            else:
                t_arrival(base + u).wait_recv()
        block = jnp.concatenate([tr[base + u] for u in range(count)], axis=1)
        rows = pl.ds(pl.multiple_of(base * LANES, LANES), count * LANES)
        for n in range(num_virt // wide):
            span = slice(n * wide, (n + 1) * wide)
            total = jnp.dot(block, c_all[rows, span], preferred_element_type=jnp.float32)
            if g > 0:
                total = total + out_sum[:, span]
            if g < len(parts) - 1:
                out_sum[:, span] = total
            else:
                for m in range(2):
                    o_ref[pl.ds(2 * n + m, tile_rows, stride=per_row), :] = total[:, m * LANES:(m + 1) * LANES]

    for copy in to_cross + lend + relay + [to_partner] + h_copies:
        copy.wait_send()
    for p in served:
        pl.when(sends(p))(t_copy(p).wait_send)


def shards_kernel(half_ints, coeffs, pair_map, tile_table):
    num_i, sblock, local_j, num_basis = half_ints.shape
    num_virt = coeffs.shape[1]
    num_pair = lax.axis_size("pair")
    local_tiles = num_pair // num_i
    tile_rows = num_virt // local_tiles
    per_row = num_virt // LANES
    num_cols = num_basis // LANES
    ints = half_ints.reshape(num_i, sblock, num_basis)
    bf16 = jnp.bfloat16
    dma = pltpu.SemaphoreType.DMA
    vmem = pl.BlockSpec(memory_space=pltpu.VMEM)
    hbm = pl.BlockSpec(memory_space=pltpu.HBM)
    ints, mine, pair_map, tile_table = (
        pltpu.with_memory_space_constraint(a, pltpu.HBM) for a in (ints, coeffs, pair_map, tile_table))
    out = pl.pallas_call(
        functools.partial(kernel, num_pair, num_i, local_tiles),
        out_shape=jax.ShapeDtypeStruct((tile_rows * per_row, LANES), jnp.float32),
        in_specs=[hbm, hbm, hbm, hbm],
        out_specs=vmem,
        scratch_shapes=[
            pltpu.SMEM(pair_map.shape, jnp.int32),
            pltpu.SMEM(tile_table.shape, jnp.int32),
            pltpu.VMEM((num_basis, num_virt), bf16),
            pltpu.VMEM((local_tiles, tile_rows, num_basis), bf16),
            pltpu.VMEM((num_pair - 1, num_i, sblock, LANES), bf16),
            pltpu.VMEM((num_pair, num_i, sblock, LANES), bf16),
            pltpu.VMEM((num_pair, tile_rows, LANES), bf16),
            pltpu.VMEM((num_cols, tile_rows, LANES), bf16),
            pltpu.VMEM((tile_rows, num_virt), jnp.float32),
            dma((num_pair,)), dma((per_row,)), dma((2,)),
            dma((per_row,)), dma((per_row,)), dma((per_row,)), dma((per_row,)), dma((per_row,)), dma((per_row,)),
            dma, dma,
            dma((num_pair - 1,)), dma((num_pair,)), dma((num_pair,)), dma((num_cols,)),
            pltpu.SemaphoreType.REGULAR,
        ],
        compiler_params=pltpu.CompilerParams(
            collective_id=0, has_side_effects=True, vmem_limit_bytes=40 * 1024 * 1024),
    )(pair_map, tile_table, ints, mine)
    return out.reshape(tile_rows, local_j, num_virt)


def shards(half_ints, coeffs, pair_map, tile_table):
    num_i, sblock, local_j, num_basis = half_ints.shape
    num_virt = coeffs.shape[1]
    num_pair = lax.axis_size("pair")
    fits = (
        num_i == 2 and local_j == 1 and lax.axis_size("occ") == 4 and num_pair == 8
        and sblock % 16 == 0 and sblock * num_pair == num_basis and num_basis == 7 * LANES
        and coeffs.shape[0] * 4 == num_basis and coeffs.shape[0] % 16 == 0
        and num_virt % (6 * LANES) == 0 and num_virt % (16 * (num_pair // num_i)) == 0
    )
    body = shards_kernel if fits else shards_general
    return body(half_ints, coeffs, pair_map, tile_table)


def solution(mesh):
    placed = (P(None, "pair", "occ", None), P("occ", None), P(), P())
    return jax.shard_map(
        shards, mesh=mesh, in_specs=placed, out_specs=P("pair", "occ", None), check_vma=False
    )
```

```python
import functools

import jax
import jax.numpy as jnp
from jax import lax
from jax.experimental import pallas as pl
from jax.experimental.pallas import tpu as pltpu
from jax.sharding import PartitionSpec as P


def shards_general(half_ints, coeffs, pair_map, tile_table):
    num_occ = half_ints.shape[0]
    sblock = half_ints.shape[1]
    local_j = half_ints.shape[2]
    num_basis = half_ints.shape[3]
    num_virt = coeffs.shape[1]
    num_pair = lax.axis_size("pair")
    tile_rows = num_occ * num_virt // num_pair
    all_coeffs = lax.all_gather(coeffs, "occ", axis=0, tiled=True)
    flat_ints = half_ints.reshape(num_occ * sblock * local_j, num_basis)
    half_mo = jnp.dot(flat_ints, all_coeffs, preferred_element_type=jnp.float32).astype(
        jnp.bfloat16
    )
    tile_id = jnp.sum(
        jnp.where(jnp.arange(num_pair) == lax.axis_index("pair"), tile_table, 0)
    )
    virt_start = tile_id * tile_rows % num_virt
    column_coeffs = lax.dynamic_slice_in_dim(all_coeffs, virt_start, tile_rows, 1)
    half_flat = half_mo.reshape(num_occ, sblock, local_j * num_virt)
    slot_occ = (tile_table * tile_rows // num_virt)[:, None, None]
    outgoing = jnp.broadcast_to(half_flat[:1], (num_pair,) + half_flat.shape[1:])
    for i in range(1, num_occ):
        outgoing = jnp.where(slot_occ == i, half_flat[i:i + 1], outgoing)
    incoming = lax.all_to_all(outgoing, "pair", split_axis=0, concat_axis=0, tiled=True)
    chosen = (pair_map[:, None] == jnp.arange(num_pair)[None, :]).astype(jnp.bfloat16)
    block_coeffs = jnp.einsum(
        "pg,gsa->psa", chosen, column_coeffs.reshape(num_pair, sblock, tile_rows),
        preferred_element_type=jnp.float32,
    ).astype(jnp.bfloat16)
    result = jnp.einsum("psa,psc->ac", block_coeffs, incoming, preferred_element_type=jnp.float32)
    return result.reshape(tile_rows, local_j, num_virt)


LANES = 128
ORDER_A = (0, 6, 1, 7, 2, 3, 4, 5)
ORDER_B = (0, 6, 1, 7, 2, 3, 4, 5)


def kernel(
    num_pair, num_i, local_tiles,
    pm_hbm, tt_hbm, h_hbm, c_hbm, o_ref,
    pm_ref, tt_ref, c_all, ct, hs, hr, ts, tr, out_sum,
    h_sem, c_sem, s_sem, x_send, x_recv, y_send, y_recv, f_send, f_recv, p_send, p_recv,
    h_send, h_recv, t_send, t_recv, ready,
):
    me = lax.axis_index("pair")
    occ = lax.axis_index("occ")
    z, y = me // 2, lax.rem(me, 2)
    core = lax.rem(occ, 2)
    num_basis, num_virt = c_all.shape
    crows = c_hbm.shape[0]
    sblock = h_hbm.shape[1]
    tile_rows = num_virt // local_tiles
    per_row = num_virt // LANES
    num_cols = num_basis // LANES
    middle = num_cols // 2
    partner = occ + 1 - 2 * core
    cross = lax.rem(occ + 2, 4)
    MESH = pl.DeviceIdType.MESH

    def column(plane, line):
        place = 2 * (lax.rem(plane + 1, 4) // 2) + lax.rem(line + core, 2)
        return middle + (2 * (plane // 2) - 1) * place

    mine = column(z, y)
    shared = mine == middle
    far_planes = (lax.rem(z + 2, 4), 3 - z)
    near_plane = z + 1 - 2 * lax.rem(z, 2)
    line_a = (lax.rem(z + 1, 4) // 2) * (1 - core) + (1 - (lax.rem(z + 1, 4) // 2)) * (1 - y)
    far = [(plane, line) for line in (line_a, 1 - line_a) for plane in far_planes]
    near = [(near_plane, line_a), (z, 1 - y), (near_plane, 1 - line_a)]
    peers = [(2 * plane + line, column(plane, line)) for plane, line in far + near]

    def remote(source, target, send, recv, where):
        return pltpu.make_async_remote_copy(
            src_ref=source, dst_ref=target, send_sem=send, recv_sem=recv,
            device_id=where, device_id_type=MESH,
        )

    barrier = pltpu.get_barrier_semaphore()
    inner = lax.rem(z + 1, 4) // 2 == 1
    outer = lax.rem(z + 1, 4) // 2 == 0
    alike = [1, 3, 5]
    unlike = [0, 2, 4, 6]
    greeted = [{"occ": partner}, {"occ": cross}] + [{"pair": peers[n][0]} for n in alike]

    def greet(semaphore, where):
        pl.semaphore_signal(semaphore, inc=1, device_id=where, device_id_type=MESH)

    for peer in greeted:
        greet(barrier, peer)

    @pl.when(inner)
    def _():
        for n in unlike:
            greet(barrier, {"pair": peers[n][0]})

    mine_rows = pl.ds(pl.multiple_of(crows * occ, crows), crows)
    cross_rows = pl.ds(pl.multiple_of(crows * cross, crows), crows)

    def cols(m):
        return pl.ds(pl.multiple_of(m * LANES, LANES), LANES)

    lent = 1
    back = per_row - lent
    given = [back * y + k for k in range(lent)]
    plain = list(range(lent, back))
    taken = [back * (1 - y) + k for k in range(lent)]
    fetched = given + plain
    arriving = fetched + taken

    def h_column(m):
        return h_hbm.at[:, :, cols(m)]

    fetch_c = [
        pltpu.make_async_copy(c_hbm.at[:, cols(m)], c_all.at[mine_rows, cols(m)], c_sem.at[k])
        for k, m in enumerate(arriving)]
    fetch_h = [
        pltpu.make_async_copy(h_column(m), hs.at[n], h_sem.at[n]) for n, (_, m) in enumerate(peers)]
    fetch_own = pltpu.make_async_copy(h_column(mine), hr.at[me], h_sem.at[len(peers)])
    fetch_pm = pltpu.make_async_copy(pm_hbm, pm_ref, s_sem.at[0])
    fetch_tt = pltpu.make_async_copy(tt_hbm, tt_ref, s_sem.at[1])
    for fetch in fetch_c + fetch_h + [fetch_own, fetch_pm, fetch_tt]:
        fetch.start()

    def passed(m, send, recv, where):
        spot = c_all.at[cross_rows, cols(m)]
        return remote(spot, spot, send, recv, where)

    to_cross = []
    for k, m in enumerate(fetched):
        spot = c_all.at[mine_rows, cols(m)]
        to_cross.append(remote(spot, spot, x_send.at[k], x_recv.at[k], {"occ": cross}))
    relay = [passed(m, f_send.at[k], f_recv.at[k], {"occ": partner}) for k, m in enumerate(arriving)]
    lend = [passed(m, y_send.at[k], y_recv.at[k], {"pair": 2 * z + 1 - y}) for k, m in enumerate(given)]
    borrow = [passed(m, y_send.at[k], y_recv.at[k], {"pair": 2 * z + 1 - y}) for k, m in enumerate(taken)]
    block = c_all.at[mine_rows, :]
    to_partner = remote(block, block, p_send, p_recv, {"occ": partner})
    h_copies = [
        remote(hs.at[n], hr.at[me], h_send.at[n], h_recv.at[me], {"pair": p}) for n, (p, _) in enumerate(peers)]
    h_arrivals = [
        remote(hs.at[n], hr.at[p], h_send.at[n], h_recv.at[p], {"pair": p}) for n, (p, _) in enumerate(peers)]

    served = [a + (b - a) * (z // 2) for a, b in zip(ORDER_A, ORDER_B)]

    def t_copy(p):
        return remote(ts.at[p], tr.at[mine], t_send.at[p], t_recv.at[mine], {"pair": p})

    def t_arrival(m):
        return remote(ts.at[0], tr.at[m], t_send.at[0], t_recv.at[m], {"pair": me})

    def send_column(n):
        fetch_h[n].wait()
        h_copies[n].start()

    def send_tile(k):
        fetch_c[k].wait()
        to_cross[k].start()


    @pl.when(inner)
    def _():
        pl.semaphore_wait(barrier, len(greeted))

    @pl.when(outer)
    def _():
        pl.semaphore_wait(barrier, len(greeted) + len(unlike))
        for n in unlike:
            greet(ready, {"pair": peers[n][0]})

    for k in range(lent):
        send_tile(k)

    @pl.when(outer)
    def _():
        for n in range(2):
            send_column(n)

    @pl.when(inner)
    def _():
        for n in alike:
            send_column(n)

    for k in range(lent, len(fetched)):
        send_tile(k)
    for fetch in fetch_c[len(fetched):]:
        fetch.wait()
    to_partner.start()

    @pl.when(outer)
    def _():
        for n in range(2, len(peers)):
            send_column(n)

    @pl.when(inner)
    def _():
        pl.semaphore_wait(ready, len(unlike))
        for n in (0, 2, 4, 6):
            send_column(n)


    def turn(m):
        row = m * LANES
        while row < (m + 1) * LANES:
            j, start = row // tile_rows, row % tile_rows
            count = min(tile_rows - start, (m + 1) * LANES - row)
            ct[j, start:start + count, :] = c_all[:, m * LANES:(m + 1) * LANES].T[row - m * LANES:row - m * LANES + count]
            row += count

    for fetch in (fetch_own, fetch_pm, fetch_tt):
        fetch.wait()
    slot = []
    for g in range(num_pair):
        found = 0
        for p in range(1, num_pair):
            found = jnp.where(pm_ref[p] == g, p, found)
        slot.append(found)
    to_partner.wait_recv()

    def turn_edge(here):
        @pl.when(here == 0)
        def _():
            for m in range(lent):
                turn(m)

        @pl.when(here == 1)
        def _():
            for m in range(back, per_row):
                turn(m)

    for k in range(lent):
        to_cross[k].wait_recv()
        lend[k].start()
        relay[k].start()
    for k in range(lent):
        relay[k].wait_recv()
    turn_edge(y)
    for k in range(max(len(plain), lent)):
        if k < len(plain):
            to_cross[lent + k].wait_recv()
            relay[lent + k].start()
        if k < lent:
            borrow[k].wait_recv()
            relay[back + k].start()
    for k in range(len(plain)):
        relay[lent + k].wait_recv()
        turn(lent + k)
    for k in range(lent):
        relay[back + k].wait_recv()
    turn_edge(1 - y)
    for copy in h_arrivals:
        copy.wait_recv()

    def tile(p):
        t = tt_ref[p]
        i = jnp.where(t >= local_tiles, 1, 0)
        block = jnp.concatenate([hr[slot[g], i] for g in range(num_pair)], axis=0)
        return jnp.dot(ct[t - local_tiles * i], block, preferred_element_type=jnp.float32).astype(jnp.bfloat16)

    def sends(p):
        away = z // 2 != p // (num_pair // 2)
        return jnp.logical_and(me != p, jnp.logical_not(jnp.logical_and(shared, away)))

    for p in served:
        @pl.when(sends(p))
        def _():
            ts[p] = tile(p)
            t_copy(p).start()
    tr[mine] = tile(me)

    own_base = (z // 2) * middle
    far_base = (1 - z // 2) * (middle + 1)
    wide = 2 * LANES
    parts = ((own_base, middle + 1), (far_base, middle))
    for g, (base, count) in enumerate(parts):
        for u in range(count):
            if g == 0:
                pl.when(base + u != mine)(t_arrival(base + u).wait_recv)
            else:
                t_arrival(base + u).wait_recv()
        block = jnp.concatenate([tr[base + u] for u in range(count)], axis=1)
        rows = pl.ds(pl.multiple_of(base * LANES, LANES), count * LANES)
        for n in range(num_virt // wide):
            span = slice(n * wide, (n + 1) * wide)
            total = jnp.dot(block, c_all[rows, span], preferred_element_type=jnp.float32)
            if g > 0:
                total = total + out_sum[:, span]
            if g < len(parts) - 1:
                out_sum[:, span] = total
            else:
                for m in range(2):
                    o_ref[pl.ds(2 * n + m, tile_rows, stride=per_row), :] = total[:, m * LANES:(m + 1) * LANES]

    for copy in to_cross + lend + relay + [to_partner] + h_copies:
        copy.wait_send()
    for p in served:
        pl.when(sends(p))(t_copy(p).wait_send)


def shards_kernel(half_ints, coeffs, pair_map, tile_table):
    num_i, sblock, local_j, num_basis = half_ints.shape
    num_virt = coeffs.shape[1]
    num_pair = lax.axis_size("pair")
    local_tiles = num_pair // num_i
    tile_rows = num_virt // local_tiles
    per_row = num_virt // LANES
    num_cols = num_basis // LANES
    ints = half_ints.reshape(num_i, sblock, num_basis)
    bf16 = jnp.bfloat16
    dma = pltpu.SemaphoreType.DMA
    vmem = pl.BlockSpec(memory_space=pltpu.VMEM)
    hbm = pl.BlockSpec(memory_space=pltpu.HBM)
    ints, mine, pair_map, tile_table = (
        pltpu.with_memory_space_constraint(a, pltpu.HBM) for a in (ints, coeffs, pair_map, tile_table))
    out = pl.pallas_call(
        functools.partial(kernel, num_pair, num_i, local_tiles),
        out_shape=jax.ShapeDtypeStruct((tile_rows * per_row, LANES), jnp.float32),
        in_specs=[hbm, hbm, hbm, hbm],
        out_specs=vmem,
        scratch_shapes=[
            pltpu.SMEM(pair_map.shape, jnp.int32),
            pltpu.SMEM(tile_table.shape, jnp.int32),
            pltpu.VMEM((num_basis, num_virt), bf16),
            pltpu.VMEM((local_tiles, tile_rows, num_basis), bf16),
            pltpu.VMEM((num_pair - 1, num_i, sblock, LANES), bf16),
            pltpu.VMEM((num_pair, num_i, sblock, LANES), bf16),
            pltpu.VMEM((num_pair, tile_rows, LANES), bf16),
            pltpu.VMEM((num_cols, tile_rows, LANES), bf16),
            pltpu.VMEM((tile_rows, num_virt), jnp.float32),
            dma((num_pair,)), dma((per_row,)), dma((2,)),
            dma((per_row,)), dma((per_row,)), dma((per_row,)), dma((per_row,)), dma((per_row,)), dma((per_row,)),
            dma, dma,
            dma((num_pair - 1,)), dma((num_pair,)), dma((num_pair,)), dma((num_cols,)),
            pltpu.SemaphoreType.REGULAR,
        ],
        compiler_params=pltpu.CompilerParams(
            collective_id=0, has_side_effects=True, vmem_limit_bytes=40 * 1024 * 1024),
    )(pair_map, tile_table, ints, mine)
    return out.reshape(tile_rows, local_j, num_virt)


def shards(half_ints, coeffs, pair_map, tile_table):
    num_i, sblock, local_j, num_basis = half_ints.shape
    num_virt = coeffs.shape[1]
    num_pair = lax.axis_size("pair")
    fits = (
        num_i == 2 and local_j == 1 and lax.axis_size("occ") == 4 and num_pair == 8
        and sblock % 16 == 0 and sblock * num_pair == num_basis and num_basis == 7 * LANES
        and coeffs.shape[0] * 4 == num_basis and coeffs.shape[0] % 16 == 0
        and num_virt % (6 * LANES) == 0 and num_virt % (16 * (num_pair // num_i)) == 0
    )
    body = shards_kernel if fits else shards_general
    return body(half_ints, coeffs, pair_map, tile_table)


def solution(mesh):
    placed = (P(None, "pair", "occ", None), P("occ", None), P(), P())
    return jax.shard_map(
        shards, mesh=mesh, in_specs=placed, out_specs=P("pair", "occ", None), check_vma=False
    )
```
